512 devices in a mesh: lists: 128 (over z, x, core), help: 4 (over y).
Axes of the slice: x: 4, y: 4, z: 16, core: 2. Of those that a mesh axis runs over, the one named last changes fastest.
Arguments:
- vectors: float32 [256, 1024, 768], P('lists', 'help'), may hold values from -6 to 6
- labels: int32 [256, 1024], P('lists', 'help'), may hold values from 0 to 1, as said below
- list_sizes: int32 [256], P('lists'), may hold values from 64 to 1024, as said below
- centroids: float32 [256, 768], P('lists'), may hold values from -4 to 4
- split_ids: int32 [64], replicated, may hold values from 0 to 255, as said below
- nearby: int32 [64, 8], replicated, may hold values from 0 to 255, as said below
- owner_map: int32 [256], replicated, may hold values from 0 to 255, as said below
- mover_source: int32 [65536], P(('lists', 'help')), may hold values from 0 to 511, as said below
- mover_dest: int32 [65536], P(('lists', 'help')), may hold values from -1 to 255, as said below
Outputs:
- gains: float32 [256, 1024], P('lists', 'help')
- arrivals: float32 [256, 512, 768], P('lists')
The draws below stay inside these ranges and needn't reach their ends.
Inputs may be any that keep to these rules, and one draw needn't show every extreme that they name: `split_ids`: distinct list ids. `nearby`: for each split, 8 distinct list ids, none equal to the split list. `owner_map`: a permutation of the slots. `list_sizes`: every list has at least two live rows; every split list has at least 576 live rows; the first slot of every index of lists that does not hold a split list holds at least 832 live rows. `labels`: row 0 of every list has label 0 and row 1 label 1. `mover_source`: distinct rows of the source device's block, live ones first. `mover_dest`: -1 exactly where the mover's source row is not live; from one device at most 2 live movers go to lists stored on one index of lists; every list slot receives at most 512 rows in all. Numbers of movers counted from these ids (per device and slot, or running totals of them) are small exact integers and may cross devices in any exact integer encoding, several to a word.
All inputs are finite; a program needn't handle non-finite values.
Results may differ from the reference program's by a relative error of at most 0.0003.
Values sent between devices are 32-bit elements; how exact they have to be, the bound alone decides.
No kernel may reach another device: no remote copies, remote signals or barrier semaphores. Data moves between devices by JAX's collectives and lax.ppermute only.
A program may use at most 64 MiB of HBM per device.

```python
import jax
import jax.numpy as jnp
from jax import lax

D = 768
LIST_DEV = 2
CAP = 1024
NEAR = 8
MOVE_DEV = 128
NLISTS = 256
SPLITS = 64
MOVERS = 65536
MOST = 2
ARRIVE_CAP = 512
N_HELP = 4


def layout(key):
    keys = jax.random.split(jax.random.fold_in(key, 7), 8)
    lists_count = NLISTS // LIST_DEV
    sources = MOVERS // MOVE_DEV
    help_count = sources // lists_count
    rows = CAP // help_count
    local = LIST_DEV * rows
    order = jax.random.permutation(keys[0], NLISTS).astype(jnp.int32)
    split_ids = order[:SPLITS]

    def near_one(k):
        return jax.random.permutation(k, NLISTS - 1)[:NEAR].astype(jnp.int32) + 1
    offsets = jax.vmap(near_one)(jax.random.split(keys[1], SPLITS))
    nearby = (split_ids[:, None] + offsets) % NLISTS
    owner = jax.random.permutation(keys[2], NLISTS).astype(jnp.int32)
    slot_list = jnp.argsort(owner).astype(jnp.int32)
    flagged = jnp.zeros((NLISTS,), jnp.int32).at[split_ids].set(1)[slot_list]
    lower = jax.random.randint(keys[3], (NLISTS,), CAP // 16, 3 * CAP // 8 + 1)
    upper = jax.random.randint(keys[4], (NLISTS,), 9 * CAP // 16, CAP + 1)
    full = jax.random.randint(keys[7], (NLISTS,), 13 * CAP // 16, CAP + 1)
    leading_slot = jnp.arange(NLISTS, dtype=jnp.int32) % LIST_DEV == 0
    sizes = jnp.where(flagged == 1, upper, jnp.where(leading_slot, full, lower))
    sizes = sizes.astype(jnp.int32).at[owner[split_ids[0]]].set(CAP)
    hottest = jax.random.randint(keys[5], (), 0, lists_count)

    def movers_of(k, device):
        ka, kb = jax.random.split(k, 2)
        lists_part = device // help_count
        help_part = device % help_count
        mine = jnp.arange(local, dtype=jnp.int32)
        slot = lists_part * LIST_DEV + mine // rows
        alive = help_part * rows + mine % rows < sizes[slot]
        live_count = jnp.sum(alive.astype(jnp.int32))
        shuffled = jax.random.permutation(ka, local).astype(jnp.int32)
        ranking = jnp.zeros((local,), jnp.int32).at[shuffled].set(mine)
        scores = jnp.where(alive, 0, local) + ranking
        source = jnp.argsort(scores)[:MOVE_DEV].astype(jnp.int32)
        tokens = jax.random.permutation(kb, lists_count * MOST).astype(jnp.int32)
        leading = jnp.argsort(jnp.where(tokens // MOST == hottest, 0, 1), stable=True)
        picked = tokens[leading][:MOVE_DEV]
        target = picked // MOST
        within = picked % MOST % LIST_DEV
        dest = slot_list[target * LIST_DEV + within]
        dest = jnp.where(jnp.arange(MOVE_DEV, dtype=jnp.int32) < live_count, dest, -1).astype(jnp.int32)
        return (source, dest)
    source_all, dest_all = jax.vmap(movers_of)(jax.random.split(keys[6], sources), jnp.arange(sources, dtype=jnp.int32))
    return (split_ids, nearby, owner, sizes, source_all.reshape(-1), dest_all.reshape(-1))


def draw_split_ids(key, part):
    return layout(key)[0]


def draw_nearby(key, part):
    return layout(key)[1]


def draw_owner_map(key, part):
    return layout(key)[2]


def draw_list_sizes(key, part):
    return layout(key)[3]


def draw_mover_source(key, part):
    return layout(key)[4]


def draw_mover_dest(key, part):
    return layout(key)[5]


def draw_labels(key, part):
    coins = jax.random.randint(jax.random.fold_in(key, 11), (NLISTS, CAP), 0, 2)
    return coins.at[:, 0].set(0).at[:, 1].set(1).astype(jnp.int32)


def draw_vectors(key, part):
    ka, kb = jax.random.split(jax.random.fold_in(key, 13), 2)
    centre = jax.random.normal(ka, (NLISTS, 1, D), jnp.float32) * 0.7
    value = centre + 0.5 * jax.random.normal(kb, (NLISTS, CAP, D), jnp.float32)
    return jnp.clip(value, -6.0, 6.0).astype(jnp.float32)


def shard_levels(key, extent, cuts, least, high):
    level, own = 1.0, jax.random.fold_in(key, 6)
    for axis_at, blocks in cuts:
        draws = jnp.exp(jax.random.uniform(jax.random.fold_in(own, axis_at), (blocks,), jnp.float32, least / len(cuts), high / len(cuts)))
        level = level * jnp.repeat(draws, extent[axis_at] // blocks).reshape([-1 if axis == axis_at else 1 for axis in range(len(extent))])
    return level


def bell_draw(key, dims, scale, most, shards=(), kind=jnp.bfloat16):
    gain = shard_levels(key, dims, shards, -0.22, 0.18) if shards else 1.0
    entries = jax.random.normal(key, dims, jnp.float32) * scale * gain
    return jnp.minimum(jnp.maximum(entries, -most), most).astype(kind)


def setup_inputs(seed: int = 0) -> dict:
    splits = jax.random.split(jax.random.key(seed), 10)
    vectors = draw_vectors(jax.random.fold_in(splits[9], 71), 0)
    labels = draw_labels(jax.random.fold_in(splits[9], 71), 0)
    list_sizes = draw_list_sizes(jax.random.fold_in(splits[9], 71), 0)
    centroids = bell_draw(splits[3], (NLISTS, D), 0.7, 4.0, ((0, 128),), jnp.float32)
    split_ids = draw_split_ids(jax.random.fold_in(splits[9], 71), 0)
    nearby = draw_nearby(jax.random.fold_in(splits[9], 71), 0)
    owner_map = draw_owner_map(jax.random.fold_in(splits[9], 71), 0)
    mover_source = draw_mover_source(jax.random.fold_in(splits[9], 71), 0)
    mover_dest = draw_mover_dest(jax.random.fold_in(splits[9], 71), 0)
    return dict(vectors=vectors, labels=labels, list_sizes=list_sizes, centroids=centroids, split_ids=split_ids, nearby=nearby, owner_map=owner_map, mover_source=mover_source, mover_dest=mover_dest)


HIGH = lax.Precision.HIGHEST


def reference(vectors, labels, list_sizes, centroids, split_ids, nearby, owner_map, mover_source, mover_dest):
    total, cap, width = vectors.shape
    rows_index = jnp.arange(cap, dtype=jnp.int32)
    valid = rows_index[None, :] < list_sizes[:, None]
    split_slots = owner_map[split_ids]
    chosen = vectors[split_slots]
    chosen_labels = labels[split_slots]
    chosen_valid = valid[split_slots]
    halves = jnp.stack([(chosen_labels == 0) & chosen_valid, (chosen_labels == 1) & chosen_valid], axis=1).astype(jnp.float32)
    sums = jnp.einsum("sac,scd->sad", halves, chosen, precision=HIGH)
    counts = jnp.sum(halves, axis=2)
    new_cent = sums / counts[:, :, None]
    cents = new_cent.reshape(-1, width)
    sq_cent = jnp.sum(cents * cents, axis=1)
    near_slots = owner_map[nearby]
    slot_ids = jnp.arange(total, dtype=jnp.int32)
    hit = jnp.any(near_slots[None, :, :] == slot_ids[:, None, None], axis=2)

    def score(args):
        block, cent, mask, okay = args
        square = jnp.sum(block * block, axis=1)
        cross = jnp.dot(block, cents.T, precision=HIGH)
        dist = square[:, None] - 2.0 * cross + sq_cent[None, :]
        far = jnp.min(jnp.where(jnp.repeat(mask, 2)[None, :], dist, 1e30), axis=1)
        own = square - 2.0 * jnp.dot(block, cent, precision=HIGH) + jnp.sum(cent * cent)
        return jnp.where(okay & jnp.any(mask), (own - far) / width, 0.0)

    gains = lax.map(score, (vectors, centroids, hit, valid))
    rows = cap // N_HELP
    count = mover_source.shape[0]
    device = jnp.arange(count, dtype=jnp.int32) // MOVE_DEV
    lists_part = device // N_HELP
    help_part = device % N_HELP
    slot = lists_part * LIST_DEV + mover_source // rows
    row = help_part * rows + mover_source % rows
    moving = vectors[slot, row]
    live_move = mover_dest >= 0
    dest = jnp.where(live_move, owner_map[jnp.maximum(mover_dest, 0)], total).astype(jnp.int32)
    order = jnp.argsort(dest, stable=True).astype(jnp.int32)
    sorted_dest = dest[order]
    starts = jnp.searchsorted(sorted_dest, jnp.arange(total + 1, dtype=jnp.int32)).astype(jnp.int32)
    rank_sorted = jnp.arange(count, dtype=jnp.int32) - starts[sorted_dest]
    position = jnp.zeros((count,), jnp.int32).at[order].set(rank_sorted)
    place = jnp.where(live_move, dest * ARRIVE_CAP + position, total * ARRIVE_CAP).astype(jnp.int32)
    arrivals = jnp.zeros((total * ARRIVE_CAP, width), jnp.float32).at[place].set(moving, mode="drop")
    return gains, arrivals.reshape(total, ARRIVE_CAP, width)
```

```python
import jax
import jax.numpy as jnp
from jax import lax
from jax.experimental import pallas as pl
from jax.experimental.pallas import tpu as pltpu
from jax.sharding import Mesh
from jax.sharding import PartitionSpec as P

LISTS = ("z", "x", "core")
HIGH = lax.Precision.HIGHEST


def exchanged(pieces, axis):
    return lax.all_to_all(pieces, axis, 0, 0, tiled=True)


def copies(shard, axis):
    length = lax.axis_size(axis)
    return exchanged(jnp.broadcast_to(shard[None], (length, *shard.shape)), axis)


def swapped(block, axis, bit):
    length = lax.axis_size(axis)
    return lax.ppermute(block, axis, [(i, i ^ bit) for i in range(length)])


def turned(block, axis, step):
    length = lax.axis_size(axis)
    return lax.ppermute(block, axis, [(i, (i + step) % length) for i in range(length)])


def doubled(block, axis):
    bit = 1
    while bit < lax.axis_size(axis):
        block = jnp.concatenate([block, swapped(block, axis, bit)], axis=0)
        bit *= 2
    return block


def place_kernel(width, total, place, own, below, above, far_low, far_high, out, image, sem):
    image[...] = jnp.zeros_like(image)
    at = 0
    for ref in (own, below, above, far_low, far_high):
        lines = ref.shape[0]
        base = at

        def body(i, carry, ref=ref, base=base, lines=lines):
            for r in range(2):
                p = place[base + r * lines + i]
                image[pl.ds(p, 1), :] = ref[i, :, r * width : (r + 1) * width]
            return carry

        lax.fori_loop(0, lines, body, 0, unroll=4)
        at += 2 * lines
    copy = pltpu.make_async_copy(image.at[pl.ds(0, total)], out, sem)
    copy.start()
    copy.wait()


def placed_rows(place, parts, width, total):
    vmem = pl.BlockSpec(memory_space=pltpu.VMEM)
    return pl.pallas_call(
        lambda *refs: place_kernel(width, total, *refs),
        out_shape=jax.ShapeDtypeStruct((total, width), jnp.float32),
        in_specs=[pl.BlockSpec(memory_space=pltpu.SMEM)] + [vmem] * len(parts),
        out_specs=pl.BlockSpec(memory_space=pl.ANY),
        scratch_shapes=[pltpu.VMEM((total + 8, width), jnp.float32), pltpu.SemaphoreType.DMA],
        name="place",
    )(place, *parts)


def local(
    vectors, labels, list_sizes, centroids, split_ids, nearby, owner_map, mover_source, mover_dest
):
    list_dev, rows, width = vectors.shape
    lists_count = lax.axis_size(LISTS)
    help_count = lax.axis_size("help")
    my_line = lax.axis_index(LISTS)
    my_help = lax.axis_index("help")
    first = my_line * list_dev
    start_row = my_help * rows
    splits = split_ids.shape[0]
    cols = width // help_count
    local_slots = first + jnp.arange(list_dev, dtype=jnp.int32)
    row_index = start_row + jnp.arange(rows, dtype=jnp.int32)
    valid = row_index[None, :] < list_sizes[:, None]
    moves = mover_source.shape[0]
    ids = jnp.arange(owner_map.shape[0], dtype=jnp.int32)
    devs = jnp.arange(lists_count, dtype=jnp.int32)
    depth = 2

    live = mover_dest >= 0
    slot = jnp.sum(
        jnp.where(mover_dest[:, None] == ids[None, :], owner_map[None, :], 0), axis=1
    )
    dev = jnp.where(live, slot // list_dev, -1)
    order = jnp.arange(moves, dtype=jnp.int32)
    same = (dev[:, None] == dev[None, :]) & (order[:, None] > order[None, :])
    rank = jnp.sum(same.astype(jnp.int32), axis=1)
    to = dev[:, None] == devs[None, :]
    picked = [to & (rank == r)[:, None] for r in range(depth)]
    codes = [
        jnp.sum(jnp.where(p, (slot % list_dev + 1)[:, None], 0), axis=0) for p in picked
    ]
    takes = [jnp.sum(jnp.where(p, mover_source[:, None], 0), axis=0) for p in picked]
    flat_rows = vectors.reshape(list_dev * rows, width)
    sent = [flat_rows[t] for t in takes]
    code_lanes = jnp.stack(codes, axis=1).astype(jnp.float32)
    bucket = jnp.concatenate([*sent, code_lanes], axis=1)[:, None, :]
    own = exchanged(bucket, LISTS)

    halves = jnp.stack([(labels == 0) & valid, (labels == 1) & valid], axis=1).astype(jnp.float32)
    partial_value = jnp.einsum("kar,krd->kad", halves, vectors, precision=HIGH)
    counts = jnp.sum(halves, axis=2)
    half = list_dev * 2
    sums = jnp.concatenate([partial_value.reshape(-1), counts.reshape(-1)])[None]
    bit = 1
    while bit < help_count:
        sums = sums + swapped(sums, "help", bit)
        bit *= 2
    means = sums[0, : half * width].reshape(half, width) / sums[0, half * width :][:, None]
    means = means.reshape(half, help_count, cols)
    part = lax.dynamic_index_in_dim(means, my_help, axis=1, keepdims=False)
    table = part.reshape(1, half * cols)
    for axis in LISTS:
        table = doubled(table, axis)
    table = table.reshape(lists_count * list_dev, 2 * cols)
    split_slots = owner_map[split_ids]
    apart = (split_slots // list_dev) ^ my_line
    x_count, core_count = lax.axis_size("x"), lax.axis_size("core")
    z_count = lax.axis_size("z")
    z_part = apart // (x_count * core_count)
    x_part = apart // core_count % x_count
    block = (apart % core_count * x_count + x_part) * z_count + z_part
    chosen = table[block * list_dev + split_slots % list_dev]
    quarters = copies(chosen.reshape(splits * 2, cols), "help")
    cents = jnp.moveaxis(quarters, 0, 1).reshape(splits * 2, width)

    sq_cent = jnp.sum(cents * cents, axis=1)
    near_slots = owner_map[nearby]
    hit = jnp.any(near_slots[None, :, :] == local_slots[:, None, None], axis=2)
    paired = jnp.repeat(hit, 2, axis=1)
    cross = jnp.einsum("krd,cd->krc", vectors, cents, precision=HIGH)
    far = jnp.min(
        jnp.where(paired[:, None, :], sq_cent[None, None, :] - 2.0 * cross, 1e30), axis=2
    )
    own_cross = jnp.einsum("krd,kd->kr", vectors, centroids, precision=HIGH)
    own_dist = jnp.sum(centroids * centroids, axis=1)[:, None] - 2.0 * own_cross
    touched = valid & jnp.any(hit, axis=1)[:, None]
    gains = jnp.where(touched, (own_dist - far) / width, 0.0)

    cut = lists_count // 2
    below = turned(own, "help", 1)
    above = turned(own, "help", -1)
    far_low = turned(below[:cut], "help", 1)
    far_high = turned(above[cut:], "help", -1)
    parts = [own, below, above, far_low, far_high]
    code_of = [p[:, 0, depth * width : depth * width + depth].T.astype(jnp.int32) for p in parts]
    got = jnp.stack([*code_of[:3], jnp.concatenate(code_of[3:], axis=1)])
    turn = jnp.array([0, -1, 1, 2], jnp.int32)
    helper = (my_help + turn) % help_count
    arrive_cap = lists_count * help_count * ((depth + list_dev - 1) // list_dev)
    total = list_dev * arrive_cap
    where_to = jnp.full(got.shape, total, jnp.int32)
    sooner = (helper[None, :] < helper[:, None])[:, :, None]
    for t in range(list_dev):
        mark = (got == t + 1).astype(jnp.int32)
        per_help = jnp.sum(mark, axis=1)
        per_line = jnp.sum(per_help, axis=0)
        ahead = jnp.sum(jnp.where(devs[None, :] < devs[:, None], per_line[None, :], 0), axis=1)
        ahead = ahead[None] + jnp.sum(jnp.where(sooner, per_help[None], 0), axis=1)
        places = jnp.stack([ahead, ahead + mark[:, 0]], axis=1)
        where_to = jnp.where(mark == 1, t * arrive_cap + places, where_to)
    place = jnp.concatenate(
        [
            where_to[:3].reshape(-1),
            where_to[3, :, :cut].reshape(-1),
            where_to[3, :, cut:].reshape(-1),
        ]
    )
    out = placed_rows(place, parts, width, total)
    return gains, out.reshape(list_dev, arrive_cap, width)


def solution(mesh):
    split = Mesh(
        mesh.devices.reshape(16, 4, 2, mesh.shape["help"]), (*LISTS, "help")
    )
    placed = (
        P(LISTS, "help", None),
        P(LISTS, "help"),
        P(LISTS),
        P(LISTS, None),
        P(),
        P(),
        P(),
        P((*LISTS, "help")),
        P((*LISTS, "help")),
    )
    return jax.shard_map(
        local,
        mesh=split,
        in_specs=placed,
        out_specs=(P(LISTS, "help"), P(LISTS, None, None)),
        check_vma=False,
    )
```

```python
import jax
import jax.numpy as jnp
from jax import lax
from jax.experimental import pallas as pl
from jax.experimental.pallas import tpu as pltpu
from jax.sharding import Mesh
from jax.sharding import PartitionSpec as P

NEAR = ("z_lo", "x", "core")
LISTS = ("z_hi", *NEAR)
LANES = 128
HIGH = lax.Precision.HIGHEST


def exchanged(pieces, axis):
    return lax.all_to_all(pieces, axis, 0, 0, tiled=True)


def copies(shard, axis):
    length = lax.axis_size(axis)
    return exchanged(jnp.broadcast_to(shard[None], (length, *shard.shape)), axis)


def turned(block, axis, step):
    length = lax.axis_size(axis)
    return lax.ppermute(block, axis, [(i, (i + step) % length) for i in range(length)])


def select_kernel(cols, depth, key, tail, out):
    lines = tail.shape[0]
    pairs = key.shape[1]
    rows = tail[:, 0, :].T
    line = lax.broadcasted_iota(jnp.int32, (lines, pairs), 0)
    pick = (line == key[...]).astype(jnp.float32)
    chosen = jnp.dot(rows, pick, precision=HIGH, preferred_element_type=jnp.float32)
    each = LANES // 4
    splits = pairs // 2
    for a in range(2):
        at = a * each
        out[:, a * splits : (a + 1) * splits] = (
            chosen[at : at + each, :splits] + chosen[at + 2 * each : at + 3 * each, splits:]
        )
    for r in range(depth):
        out[cols + 1 + r : cols + 2 + r, :] = rows[cols + 1 + r : cols + 2 + r, :]


def selected(key, got, cols, depth):
    lines, _, wide = got.shape
    last = wide // LANES - 1
    return pl.pallas_call(
        lambda *refs: select_kernel(cols, depth, *refs),
        grid=(1,),
        out_shape=jax.ShapeDtypeStruct((LANES // 4, LANES), jnp.float32),
        in_specs=[
            pl.BlockSpec(key.shape, lambda i: (0, 0)),
            pl.BlockSpec((lines, 1, LANES), lambda i: (0, 0, last)),
        ],
        out_specs=pl.BlockSpec((LANES // 4, LANES), lambda i: (0, 0)),
        name="select",
    )(key, got)


def place_kernel(width, total, place, me, own, below, above, far_low, far_high, out, image, sem):
    image[...] = jnp.zeros_like(image)
    lines = own.shape[0]
    for ref, turn, start in (
        (own, 0, 0),
        (below, 3, 0),
        (above, 1, 0),
        (far_low, 2, 0),
        (far_high, 2, lines // 2),
    ):
        base = lax.rem(me[0] + turn, 4) * (2 * lines) + start

        def body(i, carry, ref=ref, base=base):
            for r in range(2):
                p = place[base + r * lines + i]
                image[pl.ds(p, 1), :] = ref[i, :, r * width : (r + 1) * width]
            return carry

        lax.fori_loop(0, ref.shape[0], body, 0, unroll=4)
    copy = pltpu.make_async_copy(image.at[pl.ds(0, total)], out, sem)
    copy.start()
    copy.wait()


def placed_rows(place, me, parts, width, total):
    vmem = pl.BlockSpec(memory_space=pltpu.VMEM)
    smem = pl.BlockSpec(memory_space=pltpu.SMEM)
    return pl.pallas_call(
        lambda *refs: place_kernel(width, total, *refs),
        out_shape=jax.ShapeDtypeStruct((total, width), jnp.float32),
        in_specs=[smem, smem] + [vmem] * len(parts),
        out_specs=pl.BlockSpec(memory_space=pl.ANY),
        scratch_shapes=[pltpu.VMEM((total + 8, width), jnp.float32), pltpu.SemaphoreType.DMA],
        name="place",
    )(place, me, *parts)


def local(
    vectors, labels, list_sizes, centroids, split_ids, nearby, owner_map, mover_source, mover_dest
):
    list_dev, rows, width = vectors.shape
    lists_count = lax.axis_size(LISTS)
    help_count = lax.axis_size("help")
    my_line = lax.axis_index(LISTS)
    my_help = lax.axis_index("help")
    first = my_line * list_dev
    start_row = my_help * rows
    splits = split_ids.shape[0]
    local_slots = first + jnp.arange(list_dev, dtype=jnp.int32)
    row_index = start_row + jnp.arange(rows, dtype=jnp.int32)
    valid = row_index[None, :] < list_sizes[:, None]
    moves = mover_source.shape[0]
    ids = jnp.arange(owner_map.shape[0], dtype=jnp.int32)
    devs = jnp.arange(lists_count, dtype=jnp.int32)
    depth = 2

    live = mover_dest >= 0
    slot = jnp.sum(
        jnp.where(mover_dest[:, None] == ids[None, :], owner_map[None, :], 0), axis=1
    )
    dev = jnp.where(live, slot // list_dev, -1)
    order = jnp.arange(moves, dtype=jnp.int32)
    same = (dev[:, None] == dev[None, :]) & (order[:, None] > order[None, :])
    rank = jnp.sum(same.astype(jnp.int32), axis=1)
    to = dev[:, None] == devs[None, :]
    picked = [to & (rank == r)[:, None] for r in range(depth)]
    codes = [
        jnp.sum(jnp.where(p, (slot % list_dev + 1)[:, None], 0), axis=0) for p in picked
    ]
    takes = [jnp.sum(jnp.where(p, mover_source[:, None], 0), axis=0) for p in picked]
    flat_rows = vectors.reshape(list_dev * rows, width)
    sent = [flat_rows[t] for t in takes]

    halves = jnp.stack([(labels == 0) & valid, (labels == 1) & valid], axis=1).astype(jnp.float32)
    partial_value = jnp.einsum("kar,krd->kad", halves, vectors, precision=HIGH)
    counts = jnp.sum(halves, axis=2)
    chunks = lax.axis_size(NEAR)
    cols = width // chunks
    half = list_dev * 2
    lanes = jnp.moveaxis(partial_value.reshape(half, chunks, cols), 1, 0)
    lanes = jnp.concatenate(
        [
            lanes,
            jnp.broadcast_to(counts.reshape(1, half, 1), (chunks, half, 1)),
            jnp.zeros((chunks, half, LANES // half - cols - 1), jnp.float32),
        ],
        axis=2,
    ).reshape(chunks, LANES)
    lanes = jnp.tile(lanes, (lists_count // chunks, 1))
    lane = jnp.arange(LANES, dtype=jnp.int32)
    for r in range(depth):
        lanes = jnp.where(
            lane[None, :] == cols + 1 + r, codes[r].astype(jnp.float32)[:, None], lanes
        )
    bucket = jnp.concatenate([*sent, lanes], axis=1)[:, None, :]
    got = exchanged(bucket, LISTS)

    split_slots = owner_map[split_ids]
    k_ids = jnp.arange(list_dev, dtype=jnp.int32)[:, None]
    key = jnp.where(split_slots[None] % list_dev == k_ids, split_slots[None] // list_dev, -1)
    chosen = selected(key.reshape(1, list_dev * splits), got, cols, depth)
    over_help = copies(chosen, "help")
    sums = jnp.sum(over_help[:, : cols + 1], axis=0)
    got_codes = over_help[:, cols + 1 : cols + 1 + depth].astype(jnp.int32)
    means = sums[:cols] / sums[cols:]
    cents = copies(means, NEAR).reshape(width, 2 * splits)

    sq_cent = jnp.sum(cents * cents, axis=0)
    near_slots = owner_map[nearby]
    hit = jnp.any(near_slots[None, :, :] == local_slots[:, None, None], axis=2)
    paired = jnp.tile(hit, (1, 2))
    cross = jnp.einsum("krd,dc->krc", vectors, cents, precision=HIGH)
    far = jnp.min(
        jnp.where(paired[:, None, :], sq_cent[None, None, :] - 2.0 * cross, 1e30), axis=2
    )
    own_cross = jnp.einsum("krd,kd->kr", vectors, centroids, precision=HIGH)
    own_dist = jnp.sum(centroids * centroids, axis=1)[:, None] - 2.0 * own_cross
    touched = valid & jnp.any(hit, axis=1)[:, None]
    gains = jnp.where(touched, (own_dist - far) / width, 0.0)

    cut = lists_count // 2
    own = got[:, :, : depth * width]
    below = turned(own, "help", 1)
    above = turned(own, "help", -1)
    far_low = turned(below[:cut], "help", 1)
    far_high = turned(above[cut:], "help", -1)
    parts = [own, below, above, far_low, far_high]
    arrive_cap = lists_count * help_count * ((depth + list_dev - 1) // list_dev)
    total = list_dev * arrive_cap
    where_to = jnp.full(got_codes.shape, total, jnp.int32)
    helper = jnp.arange(help_count, dtype=jnp.int32)
    sooner = (helper[None, :] < helper[:, None])[:, :, None]
    for t in range(list_dev):
        mark = (got_codes == t + 1).astype(jnp.int32)
        per_help = jnp.sum(mark, axis=1)
        per_line = jnp.sum(per_help, axis=0)
        ahead = jnp.sum(jnp.where(devs[None, :] < devs[:, None], per_line[None, :], 0), axis=1)
        ahead = ahead[None] + jnp.sum(jnp.where(sooner, per_help[None], 0), axis=1)
        places = jnp.stack([ahead, ahead + mark[:, 0]], axis=1)
        where_to = jnp.where(mark == 1, t * arrive_cap + places, where_to)
    out = placed_rows(where_to.reshape(-1), my_help[None], parts, width, total)
    return gains, out.reshape(list_dev, arrive_cap, width)


def solution(mesh):
    split = Mesh(
        mesh.devices.reshape(4, 4, 4, 2, mesh.shape["help"]), (*LISTS, "help")
    )
    placed = (
        P(LISTS, "help", None),
        P(LISTS, "help"),
        P(LISTS),
        P(LISTS, None),
        P(),
        P(),
        P(),
        P((*LISTS, "help")),
        P((*LISTS, "help")),
    )
    return jax.shard_map(
        local,
        mesh=split,
        in_specs=placed,
        out_specs=(P(LISTS, "help"), P(LISTS, None, None)),
        check_vma=False,
    )
```

```python
import jax
import jax.numpy as jnp
from jax import lax
from jax.experimental import pallas as pl
from jax.experimental.pallas import tpu as pltpu
from jax.sharding import Mesh
from jax.sharding import PartitionSpec as P

NEAR = ("z_lo", "x", "core")
LISTS = ("z_hi", *NEAR)
LANES = 128
HIGH = lax.Precision.HIGHEST


def exchanged(pieces, axis):
    return lax.all_to_all(pieces, axis, 0, 0, tiled=True)


def copies(shard, axis):
    length = lax.axis_size(axis)
    return exchanged(jnp.broadcast_to(shard[None], (length, *shard.shape)), axis)


def turned(block, axis, step):
    length = lax.axis_size(axis)
    return lax.ppermute(block, axis, [(i, (i + step) % length) for i in range(length)])


def select_kernel(cols, depth, key, tail, out):
    lines = tail.shape[0]
    pairs = key.shape[1]
    rows = tail[:, 0, :].T
    line = lax.broadcasted_iota(jnp.int32, (lines, pairs), 0)
    pick = (line == key[...]).astype(jnp.float32)
    chosen = jnp.dot(rows, pick, precision=HIGH, preferred_element_type=jnp.float32)
    each = LANES // 4
    splits = pairs // 2
    own = [
        chosen[a * each : (a + 1) * each, :splits]
        + chosen[(a + 2) * each : (a + 3) * each, splits:]
        for a in range(2)
    ]
    for y in range(out.shape[0]):
        for a in range(2):
            out[y, :, a * splits : (a + 1) * splits] = own[a]
        for r in range(depth):
            at = cols + 1 + r
            out[y, at : at + 1, :] = rows[at : at + 1, :]


def selected(key, tail, cols, depth, helpers):
    vmem = pl.BlockSpec(memory_space=pltpu.VMEM)
    return pl.pallas_call(
        lambda *refs: select_kernel(cols, depth, *refs),
        out_shape=jax.ShapeDtypeStruct((helpers, LANES // 4, LANES), jnp.float32),
        in_specs=[vmem, vmem],
        out_specs=vmem,
        name="select",
    )(key, tail)


def put_rows(image, place, ref, base, start, width):
    def body(i, carry):
        for r in range(2):
            p = place[base + r, start + i]
            image[pl.ds(p, 1), :] = ref[i, :, r * width : (r + 1) * width]
        return carry

    lax.fori_loop(0, ref.shape[0], body, 0, unroll=4)


def near_kernel(width, total, skip, me, codes, own, below, above, image, place, spot, scalars, sem):
    lines = own.shape[0]
    code = jnp.concatenate([codes[y, skip : skip + 2, :] for y in range(4)], axis=0)
    before = (
        lax.broadcasted_iota(jnp.int32, (lines, lines), 0)
        < lax.broadcasted_iota(jnp.int32, (lines, lines), 1)
    ).astype(jnp.float32)
    places = jnp.full(code.shape, float(total), jnp.float32)
    for t in range(2):
        mark = (code == float(t + 1)).astype(jnp.float32)
        per_line = jnp.sum(mark, axis=0, keepdims=True)
        seen = jnp.dot(
            jnp.broadcast_to(per_line, code.shape), before, preferred_element_type=jnp.float32
        )[0:1]
        ahead = []
        for row in range(code.shape[0]):
            ahead.append(seen)
            seen = seen + mark[row : row + 1]
        ahead = jnp.concatenate(ahead, axis=0)
        places = jnp.where(mark > 0.0, ahead + float(t * total // 2), places)
    spot[...] = places.astype(jnp.int32)
    copy = pltpu.make_async_copy(spot, scalars, sem)
    copy.start()
    place[...] = spot[...]
    image[...] = jnp.zeros_like(image)
    copy.wait()
    for ref, turn in ((own, 0), (below, 3), (above, 1)):
        put_rows(image, scalars, ref, lax.rem(me[0] + turn, 4) * 2, 0, width)


def near_rows(me, codes, parts, width, total, skip):
    vmem = pl.BlockSpec(memory_space=pltpu.VMEM)
    return pl.pallas_call(
        lambda *refs: near_kernel(width, total, skip, *refs),
        out_shape=(
            pltpu.VMEM((total + 8, width), jnp.float32),
            jax.ShapeDtypeStruct((8, LANES), jnp.int32),
        ),
        in_specs=[pl.BlockSpec(memory_space=pltpu.SMEM), vmem] + [vmem] * len(parts),
        out_specs=(vmem, vmem),
        scratch_shapes=[
            pltpu.VMEM((8, LANES), jnp.int32),
            pltpu.SMEM((8, LANES), jnp.int32),
            pltpu.SemaphoreType.DMA,
        ],
        name="near",
    )(me, codes, *parts)


def far_kernel(width, total, me, place, low, high, old, image, out, sem):
    base = lax.rem(me[0] + 2, 4) * 2
    put_rows(image, place, low, base, 0, width)
    put_rows(image, place, high, base, low.shape[0], width)
    copy = pltpu.make_async_copy(image.at[pl.ds(0, total)], out, sem)
    copy.start()
    copy.wait()


def far_rows(me, place, parts, image, width, total):
    vmem = pl.BlockSpec(memory_space=pltpu.VMEM)
    smem = pl.BlockSpec(memory_space=pltpu.SMEM)
    return pl.pallas_call(
        lambda *refs: far_kernel(width, total, *refs),
        out_shape=(
            pltpu.VMEM(image.shape, jnp.float32),
            jax.ShapeDtypeStruct((total, width), jnp.float32),
        ),
        in_specs=[smem, smem] + [vmem] * (len(parts) + 1),
        out_specs=(vmem, pl.BlockSpec(memory_space=pl.ANY)),
        scratch_shapes=[pltpu.SemaphoreType.DMA],
        input_output_aliases={2 + len(parts): 0},
        name="far",
    )(me, place, *parts, image)[1]


def local(
    vectors, labels, list_sizes, centroids, split_ids, nearby, owner_map, mover_source, mover_dest
):
    list_dev, rows, width = vectors.shape
    lists_count = lax.axis_size(LISTS)
    help_count = lax.axis_size("help")
    my_line = lax.axis_index(LISTS)
    my_help = lax.axis_index("help")
    first = my_line * list_dev
    start_row = my_help * rows
    splits = split_ids.shape[0]
    local_slots = first + jnp.arange(list_dev, dtype=jnp.int32)
    row_index = start_row + jnp.arange(rows, dtype=jnp.int32)
    valid = row_index[None, :] < list_sizes[:, None]
    moves = mover_source.shape[0]
    ids = jnp.arange(owner_map.shape[0], dtype=jnp.int32)
    devs = jnp.arange(lists_count, dtype=jnp.int32)
    depth = 2

    live = mover_dest >= 0
    slot = jnp.sum(
        jnp.where(mover_dest[:, None] == ids[None, :], owner_map[None, :], 0), axis=1
    )
    dev = jnp.where(live, slot // list_dev, -1)
    order = jnp.arange(moves, dtype=jnp.int32)
    same = (dev[:, None] == dev[None, :]) & (order[:, None] > order[None, :])
    rank = jnp.sum(same.astype(jnp.int32), axis=1)
    to = dev[:, None] == devs[None, :]
    picked = [to & (rank == r)[:, None] for r in range(depth)]
    codes = [
        jnp.sum(jnp.where(p, (slot % list_dev + 1)[:, None], 0), axis=0) for p in picked
    ]
    takes = [jnp.sum(jnp.where(p, mover_source[:, None], 0), axis=0) for p in picked]
    flat_rows = vectors.reshape(list_dev * rows, width)
    sent = [flat_rows[t] for t in takes]

    halves = jnp.stack([(labels == 0) & valid, (labels == 1) & valid], axis=1).astype(jnp.float32)
    partial_value = jnp.einsum("kar,krd->kad", halves, vectors, precision=HIGH)
    counts = jnp.sum(halves, axis=2)
    chunks = lax.axis_size(NEAR)
    cols = width // chunks
    half = list_dev * 2
    lanes = jnp.moveaxis(partial_value.reshape(half, chunks, cols), 1, 0)
    lanes = jnp.concatenate(
        [
            lanes,
            jnp.broadcast_to(counts.reshape(1, half, 1), (chunks, half, 1)),
            jnp.zeros((chunks, half, LANES // half - cols - 1), jnp.float32),
        ],
        axis=2,
    ).reshape(chunks, LANES)
    lanes = jnp.tile(lanes, (lists_count // chunks, 1))
    lane = jnp.arange(LANES, dtype=jnp.int32)
    for r in range(depth):
        lanes = jnp.where(
            lane[None, :] == cols + 1 + r, codes[r].astype(jnp.float32)[:, None], lanes
        )
    bucket = jnp.concatenate([*sent, lanes], axis=1)[:, None, :]
    got = exchanged(bucket, LISTS)

    split_slots = owner_map[split_ids]
    k_ids = jnp.arange(list_dev, dtype=jnp.int32)[:, None]
    key = jnp.where(split_slots[None] % list_dev == k_ids, split_slots[None] // list_dev, -1)
    tail = got[:, :, depth * width :]
    chosen = selected(key.reshape(1, list_dev * splits), tail, cols, depth, help_count)
    over_help = exchanged(chosen, "help")
    sums = jnp.sum(over_help[:, : cols + 1], axis=0)
    means = sums[:cols] / sums[cols:]
    cents = copies(means, NEAR).reshape(width, 2 * splits)

    sq_cent = jnp.sum(cents * cents, axis=0)
    near_slots = owner_map[nearby]
    hit = jnp.any(near_slots[None, :, :] == local_slots[:, None, None], axis=2)
    paired = jnp.tile(hit, (1, 2))
    cross = jnp.einsum("krd,dc->krc", vectors, cents, precision=HIGH)
    far = jnp.min(jnp.where(paired[:, None, :], sq_cent[None, None, :] - 2.0 * cross, 1e30), axis=2)
    own_cross = jnp.einsum("krd,kd->kr", vectors, centroids, precision=HIGH)
    own_dist = jnp.sum(centroids * centroids, axis=1)[:, None] - 2.0 * own_cross
    touched = valid & jnp.any(hit, axis=1)[:, None]
    gains = jnp.where(touched, (own_dist - far) / width, 0.0)

    cut = lists_count // 2
    own = got[:, :, : depth * width]
    below = turned(own, "help", 1)
    above = turned(own, "help", -1)
    far_low = turned(below[:cut], "help", 1)
    far_high = turned(above[cut:], "help", -1)
    arrive_cap = lists_count * help_count * ((depth + list_dev - 1) // list_dev)
    total = list_dev * arrive_cap
    me = my_help[None]
    image, place = near_rows(me, over_help, [own, below, above], width, total, cols + 1)
    out = far_rows(me, place, [far_low, far_high], image, width, total)
    return gains, out.reshape(list_dev, arrive_cap, width)


def solution(mesh):
    split = Mesh(
        mesh.devices.reshape(4, 4, 4, 2, mesh.shape["help"]), (*LISTS, "help")
    )
    placed = (
        P(LISTS, "help", None),
        P(LISTS, "help"),
        P(LISTS),
        P(LISTS, None),
        P(),
        P(),
        P(),
        P((*LISTS, "help")),
        P((*LISTS, "help")),
    )

    return jax.shard_map(
        local,
        mesh=split,
        in_specs=placed,
        out_specs=(P(LISTS, "help"), P(LISTS, None, None)),
        check_vma=False,
    )
```

```python
import jax
import jax.numpy as jnp
from jax import lax
from jax.experimental import pallas as pl
from jax.experimental.pallas import tpu as pltpu
from jax.sharding import Mesh
from jax.sharding import PartitionSpec as P

NEAR = ("z_lo", "x", "core")
LISTS = ("z_hi", *NEAR)
LANES = 128
HIGH = lax.Precision.HIGHEST


def exchanged(pieces, axis):
    return lax.all_to_all(pieces, axis, 0, 0, tiled=True)


def copies(shard, axis):
    length = lax.axis_size(axis)
    return exchanged(jnp.broadcast_to(shard[None], (length, *shard.shape)), axis)


def turned(block, axis, step):
    length = lax.axis_size(axis)
    return lax.ppermute(block, axis, [(i, (i + step) % length) for i in range(length)])


def select_kernel(cols, depth, key, tail, out):
    lines = tail.shape[0]
    pairs = key.shape[1]
    rows = tail[:, 0, :].T
    line = lax.broadcasted_iota(jnp.int32, (lines, pairs), 0)
    pick = (line == key[...]).astype(jnp.float32)
    chosen = jnp.dot(rows, pick, precision=HIGH, preferred_element_type=jnp.float32)
    each = LANES // 4
    splits = pairs // 2
    own = [
        chosen[a * each : (a + 1) * each, :splits]
        + chosen[(a + 2) * each : (a + 3) * each, splits:]
        for a in range(2)
    ]
    for y in range(out.shape[0]):
        for a in range(2):
            out[y, :, a * splits : (a + 1) * splits] = own[a]
        for r in range(depth):
            at = cols + 1 + r
            out[y, at : at + 1, :] = rows[at : at + 1, :]


def selected(key, tail, cols, depth, helpers):
    vmem = pl.BlockSpec(memory_space=pltpu.VMEM)
    return pl.pallas_call(
        lambda *refs: select_kernel(cols, depth, *refs),
        out_shape=jax.ShapeDtypeStruct((helpers, LANES // 4, LANES), jnp.float32),
        in_specs=[vmem, vmem],
        out_specs=vmem,
        compiler_params=pltpu.CompilerParams(vmem_limit_bytes=4 * 2**20),
        name="select",
    )(key, tail)


def put_rows(image, place, ref, base, width):
    def body(i, carry):
        for r in range(2):
            p = place[base + r, i]
            image[pl.ds(p, 1), :] = ref[i, :, r * width : (r + 1) * width]
        return carry

    lax.fori_loop(0, ref.shape[0], body, 0, unroll=4)


def near_kernel(width, total, skip, me, codes, own, below, above, image, place, spot, scalars, sem):
    lines = own.shape[0]
    code = jnp.concatenate([codes[y, skip : skip + 2, :] for y in range(4)], axis=0)
    before = (
        lax.broadcasted_iota(jnp.int32, (lines, lines), 0)
        < lax.broadcasted_iota(jnp.int32, (lines, lines), 1)
    ).astype(jnp.float32)
    places = jnp.full(code.shape, float(total), jnp.float32)
    for t in range(2):
        mark = (code == float(t + 1)).astype(jnp.float32)
        per_line = jnp.sum(mark, axis=0, keepdims=True)
        seen = jnp.dot(
            jnp.broadcast_to(per_line, code.shape), before, preferred_element_type=jnp.float32
        )[0:1]
        ahead = []
        for row in range(code.shape[0]):
            ahead.append(seen)
            seen = seen + mark[row : row + 1]
        ahead = jnp.concatenate(ahead, axis=0)
        places = jnp.where(mark > 0.0, ahead + float(t * total // 2), places)
    spot[...] = places.astype(jnp.int32)
    copy = pltpu.make_async_copy(spot, scalars, sem)
    copy.start()
    place[...] = spot[...]
    image[...] = jnp.zeros_like(image)
    copy.wait()
    for ref, turn in ((own, 0), (below, 3), (above, 1)):
        put_rows(image, scalars, ref, lax.rem(me[0] + turn, 4) * 2, width)


def near_rows(me, codes, parts, width, total, skip):
    vmem = pl.BlockSpec(memory_space=pltpu.VMEM)
    return pl.pallas_call(
        lambda *refs: near_kernel(width, total, skip, *refs),
        out_shape=(
            pltpu.VMEM((total + 8, width), jnp.float32),
            jax.ShapeDtypeStruct((8, LANES), jnp.int32),
        ),
        in_specs=[pl.BlockSpec(memory_space=pltpu.SMEM), vmem] + [vmem] * len(parts),
        out_specs=(vmem, vmem),
        scratch_shapes=[
            pltpu.VMEM((8, LANES), jnp.int32),
            pltpu.SMEM((8, LANES), jnp.int32),
            pltpu.SemaphoreType.DMA,
        ],
        compiler_params=pltpu.CompilerParams(vmem_limit_bytes=16 * 2**20),
        name="near",
    )(me, codes, *parts)


def far_kernel(width, total, me, place, far, old, image, out, sem):
    put_rows(image, place, far, lax.rem(me[0] + 2, 4) * 2, width)
    copy = pltpu.make_async_copy(image.at[pl.ds(0, total)], out, sem)
    copy.start()
    copy.wait()


def far_rows(me, place, parts, image, width, total):
    vmem = pl.BlockSpec(memory_space=pltpu.VMEM)
    smem = pl.BlockSpec(memory_space=pltpu.SMEM)
    return pl.pallas_call(
        lambda *refs: far_kernel(width, total, *refs),
        out_shape=(
            pltpu.VMEM(image.shape, jnp.float32),
            jax.ShapeDtypeStruct((total, width), jnp.float32),
        ),
        in_specs=[smem, smem] + [vmem] * (len(parts) + 1),
        out_specs=(vmem, pl.BlockSpec(memory_space=pl.ANY)),
        scratch_shapes=[pltpu.SemaphoreType.DMA],
        input_output_aliases={2 + len(parts): 0},
        compiler_params=pltpu.CompilerParams(vmem_limit_bytes=16 * 2**20),
        name="far",
    )(me, place, *parts, image)[1]


def local(
    vectors, labels, list_sizes, centroids, split_ids, nearby, owner_map, mover_source, mover_dest
):
    list_dev, rows, width = vectors.shape
    lists_count = lax.axis_size(LISTS)
    help_count = lax.axis_size("help")
    my_line = lax.axis_index(LISTS)
    my_help = lax.axis_index("help")
    first = my_line * list_dev
    start_row = my_help * rows
    splits = split_ids.shape[0]
    local_slots = first + jnp.arange(list_dev, dtype=jnp.int32)
    row_index = start_row + jnp.arange(rows, dtype=jnp.int32)
    valid = row_index[None, :] < list_sizes[:, None]
    moves = mover_source.shape[0]
    ids = jnp.arange(owner_map.shape[0], dtype=jnp.int32)
    devs = jnp.arange(lists_count, dtype=jnp.int32)
    depth = 2

    live = mover_dest >= 0
    slot = jnp.sum(
        jnp.where(mover_dest[:, None] == ids[None, :], owner_map[None, :], 0), axis=1
    )
    dev = jnp.where(live, slot // list_dev, -1)
    order = jnp.arange(moves, dtype=jnp.int32)
    same = (dev[:, None] == dev[None, :]) & (order[:, None] > order[None, :])
    rank = jnp.sum(same.astype(jnp.int32), axis=1)
    to = dev[:, None] == devs[None, :]
    picked = [to & (rank == r)[:, None] for r in range(depth)]
    codes = [
        jnp.sum(jnp.where(p, (slot % list_dev + 1)[:, None], 0), axis=0) for p in picked
    ]
    takes = [jnp.sum(jnp.where(p, mover_source[:, None], 0), axis=0) for p in picked]
    flat_rows = vectors.reshape(list_dev * rows, width)
    sent = [flat_rows[t] for t in takes]

    halves = jnp.stack([(labels == 0) & valid, (labels == 1) & valid], axis=1).astype(jnp.float32)
    partial_value = jnp.einsum("kar,krd->kad", halves, vectors, precision=HIGH)
    counts = jnp.sum(halves, axis=2)
    chunks = lax.axis_size(NEAR)
    cols = width // chunks
    half = list_dev * 2
    lanes = jnp.moveaxis(partial_value.reshape(half, chunks, cols), 1, 0)
    lanes = jnp.concatenate(
        [
            lanes,
            jnp.broadcast_to(counts.reshape(1, half, 1), (chunks, half, 1)),
            jnp.zeros((chunks, half, LANES // half - cols - 1), jnp.float32),
        ],
        axis=2,
    ).reshape(chunks, LANES)
    lanes = jnp.tile(lanes, (lists_count // chunks, 1))
    lane = jnp.arange(LANES, dtype=jnp.int32)
    for r in range(depth):
        lanes = jnp.where(
            lane[None, :] == cols + 1 + r, codes[r].astype(jnp.float32)[:, None], lanes
        )
    bucket = jnp.concatenate([*sent, lanes], axis=1)[:, None, :]
    got = exchanged(bucket, LISTS)

    split_slots = owner_map[split_ids]
    k_ids = jnp.arange(list_dev, dtype=jnp.int32)[:, None]
    key = jnp.where(split_slots[None] % list_dev == k_ids, split_slots[None] // list_dev, -1)
    tail = got[:, :, depth * width :]
    chosen = selected(key.reshape(1, list_dev * splits), tail, cols, depth, help_count)
    over_help = exchanged(chosen, "help")
    sums = jnp.sum(over_help[:, : cols + 1], axis=0)
    means = sums[:cols] / sums[cols:]
    cents = copies(means, NEAR).reshape(width, 2 * splits)

    sq_cent = jnp.sum(cents * cents, axis=0)
    near_slots = owner_map[nearby]
    hit = jnp.any(near_slots[None, :, :] == local_slots[:, None, None], axis=2)
    own_cross = jnp.einsum("krd,kd->kr", vectors, centroids, precision=HIGH)
    own_dist = jnp.sum(centroids * centroids, axis=1)[:, None] - 2.0 * own_cross
    paired = jnp.tile(hit, (1, 2))
    cross = jnp.einsum("krd,dc->krc", vectors, cents, precision=HIGH)
    far = jnp.min(jnp.where(paired[:, None, :], sq_cent[None, None, :] - 2.0 * cross, 1e30), axis=2)
    touched = valid & jnp.any(hit, axis=1)[:, None]
    gains = jnp.where(touched, (own_dist - far) / width, 0.0)

    own = got[:, :, : depth * width]
    below = turned(own, "help", 1)
    above = turned(own, "help", -1)
    far = turned(own, "help", 2)
    arrive_cap = lists_count * help_count * ((depth + list_dev - 1) // list_dev)
    total = list_dev * arrive_cap
    me = my_help[None]
    image, place = near_rows(me, over_help, [own, below, above], width, total, cols + 1)
    out = far_rows(me, place, [far], image, width, total)
    return gains, out.reshape(list_dev, arrive_cap, width)


def solution(mesh):
    split = Mesh(
        mesh.devices.reshape(4, 4, 4, 2, mesh.shape["help"]), (*LISTS, "help")
    )
    placed = (
        P(LISTS, "help", None),
        P(LISTS, "help"),
        P(LISTS),
        P(LISTS, None),
        P(),
        P(),
        P(),
        P((*LISTS, "help")),
        P((*LISTS, "help")),
    )

    return jax.shard_map(
        local,
        mesh=split,
        in_specs=placed,
        out_specs=(P(LISTS, "help"), P(LISTS, None, None)),
        check_vma=False,
    )
```

```python
import jax
import jax.numpy as jnp
from jax import lax
from jax.experimental import pallas as pl
from jax.experimental.pallas import tpu as pltpu
from jax.sharding import Mesh
from jax.sharding import PartitionSpec as P

NEAR = ("z_lo", "x", "core")
LISTS = ("z_hi", *NEAR)
LANES = 128
HIGH = lax.Precision.HIGHEST


def exchanged(pieces, axis):
    return lax.all_to_all(pieces, axis, 0, 0, tiled=True)


def copies(shard, axis):
    length = lax.axis_size(axis)
    return exchanged(jnp.broadcast_to(shard[None], (length, *shard.shape)), axis)


def turned(block, axis, step):
    length = lax.axis_size(axis)
    return lax.ppermute(block, axis, [(i, (i + step) % length) for i in range(length)])


def select_kernel(cols, depth, key, tail, out):
    lines = tail.shape[0]
    pairs = key.shape[1]
    rows = tail[:, 0, :].T
    line = lax.broadcasted_iota(jnp.int32, (lines, pairs), 0)
    pick = (line == key[...]).astype(jnp.float32)
    chosen = jnp.dot(rows, pick, precision=HIGH, preferred_element_type=jnp.float32)
    each = LANES // 4
    splits = pairs // 2
    own = [
        chosen[a * each : (a + 1) * each, :splits]
        + chosen[(a + 2) * each : (a + 3) * each, splits:]
        for a in range(2)
    ]
    for y in range(out.shape[0]):
        for a in range(2):
            out[y, :, a * splits : (a + 1) * splits] = own[a]
        for r in range(depth):
            at = cols + 1 + r
            out[y, at : at + 1, :] = rows[at : at + 1, :]


def selected(key, tail, cols, depth, helpers):
    vmem = pl.BlockSpec(memory_space=pltpu.VMEM)
    return pl.pallas_call(
        lambda *refs: select_kernel(cols, depth, *refs),
        out_shape=jax.ShapeDtypeStruct((helpers, LANES // 4, LANES), jnp.float32),
        in_specs=[vmem, vmem],
        out_specs=vmem,
        compiler_params=pltpu.CompilerParams(vmem_limit_bytes=4 * 2**20),
        name="select",
    )(key, tail)


def put_rows(image, place, ref, base, start, width):
    def body(i, carry):
        for r in range(2):
            p = place[base + r, start + i]
            image[pl.ds(p, 1), :] = ref[i, :, r * width : (r + 1) * width]
        return carry

    lax.fori_loop(0, ref.shape[0], body, 0, unroll=4)


def near_kernel(width, total, skip, me, codes, *refs):
    *parts, image, place, spot, scalars, sem = refs
    lines = codes.shape[2]
    code = jnp.concatenate([codes[y, skip : skip + 2, :] for y in range(4)], axis=0)
    before = (
        lax.broadcasted_iota(jnp.int32, (lines, lines), 0)
        < lax.broadcasted_iota(jnp.int32, (lines, lines), 1)
    ).astype(jnp.float32)
    places = jnp.full(code.shape, float(total), jnp.float32)
    for t in range(2):
        mark = (code == float(t + 1)).astype(jnp.float32)
        per_line = jnp.sum(mark, axis=0, keepdims=True)
        seen = jnp.dot(
            jnp.broadcast_to(per_line, code.shape), before, preferred_element_type=jnp.float32
        )[0:1]
        ahead = []
        for row in range(code.shape[0]):
            ahead.append(seen)
            seen = seen + mark[row : row + 1]
        ahead = jnp.concatenate(ahead, axis=0)
        places = jnp.where(mark > 0.0, ahead + float(t * total // 2), places)
    spot[...] = places.astype(jnp.int32)
    copy = pltpu.make_async_copy(spot, scalars, sem)
    copy.start()
    place[...] = spot[...]
    image[...] = jnp.zeros_like(image)
    copy.wait()
    for at, ref in enumerate(parts):
        base = lax.rem(me[0] + (0, 3, 1)[at // 2], 4) * 2
        put_rows(image, scalars, ref, base, at % 2 * (lines // 2), width)


def near_rows(me, codes, parts, width, total, skip):
    vmem = pl.BlockSpec(memory_space=pltpu.VMEM)
    return pl.pallas_call(
        lambda *refs: near_kernel(width, total, skip, *refs),
        out_shape=(
            pltpu.VMEM((total + 8, width), jnp.float32),
            jax.ShapeDtypeStruct((8, LANES), jnp.int32),
        ),
        in_specs=[pl.BlockSpec(memory_space=pltpu.SMEM), vmem] + [vmem] * len(parts),
        out_specs=(vmem, vmem),
        scratch_shapes=[
            pltpu.VMEM((8, LANES), jnp.int32),
            pltpu.SMEM((8, LANES), jnp.int32),
            pltpu.SemaphoreType.DMA,
        ],
        compiler_params=pltpu.CompilerParams(vmem_limit_bytes=16 * 2**20),
        name="near",
    )(me, codes, *parts)


def far_kernel(width, total, me, place, low, high, old, image, out, sem):
    base = lax.rem(me[0] + 2, 4) * 2
    put_rows(image, place, low, base, 0, width)
    put_rows(image, place, high, base, low.shape[0], width)
    copy = pltpu.make_async_copy(image.at[pl.ds(0, total)], out, sem)
    copy.start()
    copy.wait()


def far_rows(me, place, parts, image, width, total):
    vmem = pl.BlockSpec(memory_space=pltpu.VMEM)
    smem = pl.BlockSpec(memory_space=pltpu.SMEM)
    return pl.pallas_call(
        lambda *refs: far_kernel(width, total, *refs),
        out_shape=(
            pltpu.VMEM(image.shape, jnp.float32),
            jax.ShapeDtypeStruct((total, width), jnp.float32),
        ),
        in_specs=[smem, smem] + [vmem] * (len(parts) + 1),
        out_specs=(vmem, pl.BlockSpec(memory_space=pl.ANY)),
        scratch_shapes=[pltpu.SemaphoreType.DMA],
        input_output_aliases={2 + len(parts): 0},
        compiler_params=pltpu.CompilerParams(vmem_limit_bytes=16 * 2**20),
        name="far",
    )(me, place, *parts, image)[1]


def local(
    vectors, labels, list_sizes, centroids, split_ids, nearby, owner_map, mover_source, mover_dest
):
    list_dev, rows, width = vectors.shape
    lists_count = lax.axis_size(LISTS)
    help_count = lax.axis_size("help")
    my_line = lax.axis_index(LISTS)
    my_help = lax.axis_index("help")
    first = my_line * list_dev
    start_row = my_help * rows
    splits = split_ids.shape[0]
    local_slots = first + jnp.arange(list_dev, dtype=jnp.int32)
    row_index = start_row + jnp.arange(rows, dtype=jnp.int32)
    valid = row_index[None, :] < list_sizes[:, None]
    moves = mover_source.shape[0]
    ids = jnp.arange(owner_map.shape[0], dtype=jnp.int32)
    devs = jnp.arange(lists_count, dtype=jnp.int32)
    depth = 2

    live = mover_dest >= 0
    slot = jnp.sum(
        jnp.where(mover_dest[:, None] == ids[None, :], owner_map[None, :], 0), axis=1
    )
    dev = jnp.where(live, slot // list_dev, -1)
    order = jnp.arange(moves, dtype=jnp.int32)
    same = (dev[:, None] == dev[None, :]) & (order[:, None] > order[None, :])
    rank = jnp.sum(same.astype(jnp.int32), axis=1)
    to = dev[:, None] == devs[None, :]
    picked = [to & (rank == r)[:, None] for r in range(depth)]
    codes = [
        jnp.sum(jnp.where(p, (slot % list_dev + 1)[:, None], 0), axis=0) for p in picked
    ]
    takes = [jnp.sum(jnp.where(p, mover_source[:, None], 0), axis=0) for p in picked]
    flat_rows = vectors.reshape(list_dev * rows, width)
    sent = [flat_rows[t] for t in takes]

    halves = jnp.stack([(labels == 0) & valid, (labels == 1) & valid], axis=1).astype(jnp.float32)
    partial_value = jnp.einsum("kar,krd->kad", halves, vectors, precision=HIGH)
    counts = jnp.sum(halves, axis=2)
    chunks = lax.axis_size(NEAR)
    cols = width // chunks
    half = list_dev * 2
    lanes = jnp.moveaxis(partial_value.reshape(half, chunks, cols), 1, 0)
    lanes = jnp.concatenate(
        [
            lanes,
            jnp.broadcast_to(counts.reshape(1, half, 1), (chunks, half, 1)),
            jnp.zeros((chunks, half, LANES // half - cols - 1), jnp.float32),
        ],
        axis=2,
    ).reshape(chunks, LANES)
    lanes = jnp.tile(lanes, (lists_count // chunks, 1))
    lane = jnp.arange(LANES, dtype=jnp.int32)
    for r in range(depth):
        lanes = jnp.where(
            lane[None, :] == cols + 1 + r, codes[r].astype(jnp.float32)[:, None], lanes
        )
    bucket = jnp.concatenate([*sent, lanes], axis=1)[:, None, :]
    got = exchanged(bucket, LISTS)

    split_slots = owner_map[split_ids]
    k_ids = jnp.arange(list_dev, dtype=jnp.int32)[:, None]
    key = jnp.where(split_slots[None] % list_dev == k_ids, split_slots[None] // list_dev, -1)
    tail = got[:, :, depth * width :]
    chosen = selected(key.reshape(1, list_dev * splits), tail, cols, depth, help_count)
    over_help = exchanged(chosen, "help")
    sums = jnp.sum(over_help[:, : cols + 1], axis=0)
    means = sums[:cols] / sums[cols:]
    cents = copies(means, NEAR).reshape(width, 2 * splits)

    near_slots = owner_map[nearby]
    hit = jnp.any(near_slots[None, :, :] == local_slots[:, None, None], axis=2)
    own_cross = jnp.einsum("krd,kd->kr", vectors, centroids, precision=HIGH)
    own_dist = jnp.sum(centroids * centroids, axis=1)[:, None] - 2.0 * own_cross
    paired = jnp.tile(hit, (1, 2))
    sq_cent = jnp.sum(cents * cents, axis=0)
    cross = jnp.einsum("krd,dc->krc", vectors, cents, precision=lax.Precision.HIGH)
    far = jnp.min(jnp.where(paired[:, None, :], sq_cent[None, None, :] - 2.0 * cross, 1e30), axis=2)
    touched = valid & jnp.any(hit, axis=1)[:, None]
    gains = jnp.where(touched, (own_dist - far) / width, 0.0)

    cut = lists_count // 2
    low, high = got[:cut, :, : depth * width], got[cut:, :, : depth * width]
    below_low = turned(low, "help", 1)
    above_high = turned(high, "help", -1)
    below_high = turned(high, "help", 1)
    above_low = turned(low, "help", -1)
    far_low = turned(below_low, "help", 1)
    far_high = turned(above_high, "help", -1)
    arrive_cap = lists_count * help_count * ((depth + list_dev - 1) // list_dev)
    total = list_dev * arrive_cap
    me = my_help[None]
    image, place = near_rows(me, over_help, [low, high, below_low, below_high, above_low, above_high], width, total, cols + 1)
    out = far_rows(me, place, [far_low, far_high], image, width, total)
    return gains, out.reshape(list_dev, arrive_cap, width)


def solution(mesh):
    split = Mesh(
        mesh.devices.reshape(4, 4, 4, 2, mesh.shape["help"]), (*LISTS, "help")
    )
    placed = (
        P(LISTS, "help", None),
        P(LISTS, "help"),
        P(LISTS),
        P(LISTS, None),
        P(),
        P(),
        P(),
        P((*LISTS, "help")),
        P((*LISTS, "help")),
    )

    return jax.shard_map(
        local,
        mesh=split,
        in_specs=placed,
        out_specs=(P(LISTS, "help"), P(LISTS, None, None)),
        check_vma=False,
    )
```

```python
import jax
import jax.numpy as jnp
from jax import lax
from jax.experimental import pallas as pl
from jax.experimental.pallas import tpu as pltpu
from jax.sharding import Mesh
from jax.sharding import PartitionSpec as P

NEAR = ("z_lo", "x", "core")
LISTS = ("z_hi", *NEAR)
LANES = 128
HIGH = lax.Precision.HIGHEST


def exchanged(pieces, axis):
    return lax.all_to_all(pieces, axis, 0, 0, tiled=True)


def copies(shard, axis):
    length = lax.axis_size(axis)
    return exchanged(jnp.broadcast_to(shard[None], (length, *shard.shape)), axis)


def turned(block, axis, step):
    length = lax.axis_size(axis)
    return lax.ppermute(block, axis, [(i, (i + step) % length) for i in range(length)])


def select_kernel(cols, depth, key, tail, out):
    lines = tail.shape[0]
    pairs = key.shape[1]
    rows = tail[:, 0, :].T
    line = lax.broadcasted_iota(jnp.int32, (lines, pairs), 0)
    pick = (line == key[...]).astype(jnp.float32)
    chosen = jnp.dot(rows, pick, precision=HIGH, preferred_element_type=jnp.float32)
    each = LANES // 4
    splits = pairs // 2
    own = [
        chosen[a * each : (a + 1) * each, :splits]
        + chosen[(a + 2) * each : (a + 3) * each, splits:]
        for a in range(2)
    ]
    for y in range(out.shape[0]):
        for a in range(2):
            out[y, :, a * splits : (a + 1) * splits] = own[a]
        for r in range(depth):
            at = cols + 1 + r
            out[y, at : at + 1, :] = rows[at : at + 1, :]


def selected(key, tail, cols, depth, helpers):
    vmem = pl.BlockSpec(memory_space=pltpu.VMEM)
    return pl.pallas_call(
        lambda *refs: select_kernel(cols, depth, *refs),
        out_shape=jax.ShapeDtypeStruct((helpers, LANES // 4, LANES), jnp.float32),
        in_specs=[vmem, vmem],
        out_specs=vmem,
        compiler_params=pltpu.CompilerParams(vmem_limit_bytes=4 * 2**20),
        name="select",
    )(key, tail)


def halved(values):
    high = values.astype(jnp.bfloat16)
    return high, (values - high.astype(jnp.float32)).astype(jnp.bfloat16)


def score_kernel(vectors, cents, penalty, own, touched, out):
    table = cents[...]
    base = jnp.sum(table * table, axis=0, keepdims=True)
    high, low = halved(table)
    for k in range(vectors.shape[0]):
        rows_high, rows_low = halved(vectors[k])

        def product(left, right):
            return jnp.dot(left, right, preferred_element_type=jnp.float32)

        cross = product(rows_high, low) + product(rows_low, high) + product(rows_high, high)
        dist = base + penalty[k : k + 1, :] - 2.0 * cross
        least = jnp.min(dist.T, axis=0, keepdims=True)
        gain = (own[k : k + 1, :] - least) / vectors.shape[2]
        out[k : k + 1, :] = jnp.where(touched[k : k + 1, :] > 0.0, gain, 0.0)


def scored(vectors, cents, penalty, own, touched):
    vmem = pl.BlockSpec(memory_space=pltpu.VMEM)
    return pl.pallas_call(
        score_kernel,
        out_shape=jax.ShapeDtypeStruct(own.shape, jnp.float32),
        in_specs=[vmem] * 5,
        out_specs=vmem,
        compiler_params=pltpu.CompilerParams(vmem_limit_bytes=16 * 2**20),
        name="score",
    )(vectors, cents, penalty, own, touched)


def put_rows(image, place, ref, base, start, width):
    def body(i, carry):
        for r in range(2):
            p = place[base + r, start + i]
            image[pl.ds(p, 1), :] = ref[i, :, r * width : (r + 1) * width]
        return carry

    lax.fori_loop(0, ref.shape[0], body, 0, unroll=4)


def near_kernel(width, total, skip, me, codes, *refs):
    *parts, image, place, spot, scalars, sem = refs
    lines = codes.shape[2]
    code = jnp.concatenate([codes[y, skip : skip + 2, :] for y in range(4)], axis=0)
    before = (
        lax.broadcasted_iota(jnp.int32, (lines, lines), 0)
        < lax.broadcasted_iota(jnp.int32, (lines, lines), 1)
    ).astype(jnp.float32)
    places = jnp.full(code.shape, float(total), jnp.float32)
    for t in range(2):
        mark = (code == float(t + 1)).astype(jnp.float32)
        per_line = jnp.sum(mark, axis=0, keepdims=True)
        seen = jnp.dot(
            jnp.broadcast_to(per_line, code.shape), before, preferred_element_type=jnp.float32
        )[0:1]
        ahead = []
        for row in range(code.shape[0]):
            ahead.append(seen)
            seen = seen + mark[row : row + 1]
        ahead = jnp.concatenate(ahead, axis=0)
        places = jnp.where(mark > 0.0, ahead + float(t * total // 2), places)
    spot[...] = places.astype(jnp.int32)
    copy = pltpu.make_async_copy(spot, scalars, sem)
    copy.start()
    place[...] = spot[...]
    image[...] = jnp.zeros_like(image)
    copy.wait()
    for at, ref in enumerate(parts):
        base = lax.rem(me[0] + (0, 3, 1)[at // 2], 4) * 2
        put_rows(image, scalars, ref, base, at % 2 * (lines // 2), width)


def near_rows(me, codes, parts, width, total, skip):
    vmem = pl.BlockSpec(memory_space=pltpu.VMEM)
    return pl.pallas_call(
        lambda *refs: near_kernel(width, total, skip, *refs),
        out_shape=(
            pltpu.VMEM((total + 8, width), jnp.float32),
            jax.ShapeDtypeStruct((8, LANES), jnp.int32),
        ),
        in_specs=[pl.BlockSpec(memory_space=pltpu.SMEM), vmem] + [vmem] * len(parts),
        out_specs=(vmem, vmem),
        scratch_shapes=[
            pltpu.VMEM((8, LANES), jnp.int32),
            pltpu.SMEM((8, LANES), jnp.int32),
            pltpu.SemaphoreType.DMA,
        ],
        compiler_params=pltpu.CompilerParams(vmem_limit_bytes=16 * 2**20),
        name="near",
    )(me, codes, *parts)


def far_kernel(width, total, me, place, low, high, old, image, out, sem):
    base = lax.rem(me[0] + 2, 4) * 2
    put_rows(image, place, low, base, 0, width)
    put_rows(image, place, high, base, low.shape[0], width)
    copy = pltpu.make_async_copy(image.at[pl.ds(0, total)], out, sem)
    copy.start()
    copy.wait()


def far_rows(me, place, parts, image, width, total):
    vmem = pl.BlockSpec(memory_space=pltpu.VMEM)
    smem = pl.BlockSpec(memory_space=pltpu.SMEM)
    return pl.pallas_call(
        lambda *refs: far_kernel(width, total, *refs),
        out_shape=(
            pltpu.VMEM(image.shape, jnp.float32),
            jax.ShapeDtypeStruct((total, width), jnp.float32),
        ),
        in_specs=[smem, smem] + [vmem] * (len(parts) + 1),
        out_specs=(vmem, pl.BlockSpec(memory_space=pl.ANY)),
        scratch_shapes=[pltpu.SemaphoreType.DMA],
        input_output_aliases={2 + len(parts): 0},
        compiler_params=pltpu.CompilerParams(vmem_limit_bytes=16 * 2**20),
        name="far",
    )(me, place, *parts, image)[1]


def local(
    vectors, labels, list_sizes, centroids, split_ids, nearby, owner_map, mover_source, mover_dest
):
    list_dev, rows, width = vectors.shape
    lists_count = lax.axis_size(LISTS)
    help_count = lax.axis_size("help")
    my_line = lax.axis_index(LISTS)
    my_help = lax.axis_index("help")
    first = my_line * list_dev
    start_row = my_help * rows
    splits = split_ids.shape[0]
    local_slots = first + jnp.arange(list_dev, dtype=jnp.int32)
    row_index = start_row + jnp.arange(rows, dtype=jnp.int32)
    valid = row_index[None, :] < list_sizes[:, None]
    moves = mover_source.shape[0]
    ids = jnp.arange(owner_map.shape[0], dtype=jnp.int32)
    devs = jnp.arange(lists_count, dtype=jnp.int32)
    depth = 2

    live = mover_dest >= 0
    slot = jnp.sum(
        jnp.where(mover_dest[:, None] == ids[None, :], owner_map[None, :], 0), axis=1
    )
    dev = jnp.where(live, slot // list_dev, -1)
    order = jnp.arange(moves, dtype=jnp.int32)
    same = (dev[:, None] == dev[None, :]) & (order[:, None] > order[None, :])
    rank = jnp.sum(same.astype(jnp.int32), axis=1)
    to = dev[:, None] == devs[None, :]
    picked = [to & (rank == r)[:, None] for r in range(depth)]
    codes = [
        jnp.sum(jnp.where(p, (slot % list_dev + 1)[:, None], 0), axis=0) for p in picked
    ]
    takes = [jnp.sum(jnp.where(p, mover_source[:, None], 0), axis=0) for p in picked]
    flat_rows = vectors.reshape(list_dev * rows, width)
    sent = [flat_rows[t] for t in takes]

    halves = jnp.stack([(labels == 0) & valid, (labels == 1) & valid], axis=1).astype(jnp.float32)
    partial_value = jnp.einsum("kar,krd->kad", halves, vectors, precision=HIGH)
    counts = jnp.sum(halves, axis=2)
    chunks = lax.axis_size(NEAR)
    cols = width // chunks
    half = list_dev * 2
    lanes = jnp.moveaxis(partial_value.reshape(half, chunks, cols), 1, 0)
    lanes = jnp.concatenate(
        [
            lanes,
            jnp.broadcast_to(counts.reshape(1, half, 1), (chunks, half, 1)),
            jnp.zeros((chunks, half, LANES // half - cols - 1), jnp.float32),
        ],
        axis=2,
    ).reshape(chunks, LANES)
    lanes = jnp.tile(lanes, (lists_count // chunks, 1))
    lane = jnp.arange(LANES, dtype=jnp.int32)
    for r in range(depth):
        lanes = jnp.where(
            lane[None, :] == cols + 1 + r, codes[r].astype(jnp.float32)[:, None], lanes
        )
    bucket = jnp.concatenate([*sent, lanes], axis=1)[:, None, :]
    got = exchanged(bucket, LISTS)

    split_slots = owner_map[split_ids]
    k_ids = jnp.arange(list_dev, dtype=jnp.int32)[:, None]
    key = jnp.where(split_slots[None] % list_dev == k_ids, split_slots[None] // list_dev, -1)
    tail = got[:, :, depth * width :]
    chosen = selected(key.reshape(1, list_dev * splits), tail, cols, depth, help_count)
    over_help = exchanged(chosen, "help")
    sums = jnp.sum(over_help[:, : cols + 1], axis=0)
    means = sums[:cols] / sums[cols:]
    cents = copies(means, NEAR).reshape(width, 2 * splits)

    near_slots = owner_map[nearby]
    hit = jnp.any(near_slots[None, :, :] == local_slots[:, None, None], axis=2)
    penalty = jnp.tile(jnp.where(hit, 0.0, 1e30), (1, 2))
    own_cross = jnp.einsum("krd,kd->kr", vectors, centroids, precision=HIGH)
    own_dist = jnp.sum(centroids * centroids, axis=1)[:, None] - 2.0 * own_cross
    touched = (valid & jnp.any(hit, axis=1)[:, None]).astype(jnp.float32)
    gains = scored(vectors, cents, penalty, own_dist, touched)

    cut = lists_count // 2
    low, high = got[:cut, :, : depth * width], got[cut:, :, : depth * width]
    below_low = turned(low, "help", 1)
    above_high = turned(high, "help", -1)
    below_high = turned(high, "help", 1)
    above_low = turned(low, "help", -1)
    far_low = turned(below_low, "help", 1)
    far_high = turned(above_high, "help", -1)
    arrive_cap = lists_count * help_count * ((depth + list_dev - 1) // list_dev)
    total = list_dev * arrive_cap
    me = my_help[None]
    image, place = near_rows(me, over_help, [low, high, below_low, below_high, above_low, above_high], width, total, cols + 1)
    out = far_rows(me, place, [far_low, far_high], image, width, total)
    return gains, out.reshape(list_dev, arrive_cap, width)


def solution(mesh):
    split = Mesh(
        mesh.devices.reshape(4, 4, 4, 2, mesh.shape["help"]), (*LISTS, "help")
    )
    placed = (
        P(LISTS, "help", None),
        P(LISTS, "help"),
        P(LISTS),
        P(LISTS, None),
        P(),
        P(),
        P(),
        P((*LISTS, "help")),
        P((*LISTS, "help")),
    )

    return jax.shard_map(
        local,
        mesh=split,
        in_specs=placed,
        out_specs=(P(LISTS, "help"), P(LISTS, None, None)),
        check_vma=False,
    )
```

```python
import jax
import jax.numpy as jnp
from jax import lax
from jax.experimental import pallas as pl
from jax.experimental.pallas import tpu as pltpu
from jax.sharding import Mesh
from jax.sharding import PartitionSpec as P

NEAR = ("z_lo", "x", "core")
LISTS = ("z_hi", *NEAR)
LANES = 128
FAR = 1e30
HIGH = lax.Precision.HIGHEST


def exchanged(pieces, axis):
    return lax.all_to_all(pieces, axis, 0, 0, tiled=True)


def copies(shard, axis):
    length = lax.axis_size(axis)
    return exchanged(jnp.broadcast_to(shard[None], (length, *shard.shape)), axis)


def turned(block, axis, step):
    length = lax.axis_size(axis)
    return lax.ppermute(block, axis, [(i, (i + step) % length) for i in range(length)])


def select_kernel(cols, depth, key, tail, out):
    lines = tail.shape[0]
    pairs = key.shape[1]
    rows = tail[:, 0, :].T
    line = lax.broadcasted_iota(jnp.int32, (lines, pairs), 0)
    pick = (line == key[...]).astype(jnp.float32)
    chosen = jnp.dot(rows, pick, precision=HIGH, preferred_element_type=jnp.float32)
    each = LANES // 4
    splits = pairs // 2
    own = [
        chosen[a * each : (a + 1) * each, :splits]
        + chosen[(a + 2) * each : (a + 3) * each, splits:]
        for a in range(2)
    ]
    for y in range(out.shape[0]):
        for a in range(2):
            out[y, :, a * splits : (a + 1) * splits] = own[a]
        for r in range(depth):
            at = cols + 1 + r
            out[y, at : at + 1, :] = rows[at : at + 1, :]


def selected(key, tail, cols, depth, helpers):
    vmem = pl.BlockSpec(memory_space=pltpu.VMEM)
    return pl.pallas_call(
        lambda *refs: select_kernel(cols, depth, *refs),
        out_shape=jax.ShapeDtypeStruct((helpers, LANES // 4, LANES), jnp.float32),
        in_specs=[vmem, vmem],
        out_specs=vmem,
        compiler_params=pltpu.CompilerParams(vmem_limit_bytes=4 * 2**20),
        name="select",
    )(key, tail)


def halved(values):
    high = values.astype(jnp.bfloat16)
    return high, (values - high.astype(jnp.float32)).astype(jnp.bfloat16)


def score_kernel(vectors, cents, penalty, own, live, out):
    table = cents[...]
    base = jnp.sum(table * table, axis=0, keepdims=True)
    high, low = halved(table)
    for k in range(vectors.shape[0]):
        rows_high, rows_low = halved(vectors[k])

        def product(left, right):
            return jnp.dot(left, right, preferred_element_type=jnp.float32)

        cross = product(rows_high, low) + product(rows_low, high) + product(rows_high, high)
        dist = base + penalty[k : k + 1, :] - 2.0 * cross
        least = jnp.min(dist.T, axis=0, keepdims=True)
        gain = (own[k : k + 1, :] - least) / vectors.shape[2]
        near = least < 0.5 * FAR
        out[k : k + 1, :] = jnp.where((live[k : k + 1, :] > 0.0) & near, gain, 0.0)


def scored(vectors, cents, penalty, own, live):
    vmem = pl.BlockSpec(memory_space=pltpu.VMEM)
    return pl.pallas_call(
        score_kernel,
        out_shape=jax.ShapeDtypeStruct(own.shape, jnp.float32),
        in_specs=[vmem] * 5,
        out_specs=vmem,
        compiler_params=pltpu.CompilerParams(vmem_limit_bytes=16 * 2**20),
        name="score",
    )(vectors, cents, penalty, own, live)


def put_rows(image, place, ref, base, start, width):
    def body(i, carry):
        for r in range(2):
            p = place[base + r, start + i]
            image[pl.ds(p, 1), :] = ref[i, :, r * width : (r + 1) * width]
        return carry

    lax.fori_loop(0, ref.shape[0], body, 0, unroll=4)


def near_kernel(width, total, skip, me, codes, *refs):
    *parts, image, place, spot, scalars, sem = refs
    lines = codes.shape[2]
    code = jnp.concatenate([codes[y, skip : skip + 2, :] for y in range(4)], axis=0)
    before = (
        lax.broadcasted_iota(jnp.int32, (lines, lines), 0)
        < lax.broadcasted_iota(jnp.int32, (lines, lines), 1)
    ).astype(jnp.float32)
    places = jnp.full(code.shape, float(total), jnp.float32)
    for t in range(2):
        mark = (code == float(t + 1)).astype(jnp.float32)
        per_line = jnp.sum(mark, axis=0, keepdims=True)
        seen = jnp.dot(
            jnp.broadcast_to(per_line, code.shape), before, preferred_element_type=jnp.float32
        )[0:1]
        ahead = []
        for row in range(code.shape[0]):
            ahead.append(seen)
            seen = seen + mark[row : row + 1]
        ahead = jnp.concatenate(ahead, axis=0)
        places = jnp.where(mark > 0.0, ahead + float(t * total // 2), places)
    spot[...] = places.astype(jnp.int32)
    copy = pltpu.make_async_copy(spot, scalars, sem)
    copy.start()
    place[...] = spot[...]
    image[...] = jnp.zeros_like(image)
    copy.wait()
    for at, ref in enumerate(parts):
        base = lax.rem(me[0] + (0, 3, 1)[at // 2], 4) * 2
        put_rows(image, scalars, ref, base, at % 2 * (lines // 2), width)


def near_rows(me, codes, parts, width, total, skip):
    vmem = pl.BlockSpec(memory_space=pltpu.VMEM)
    return pl.pallas_call(
        lambda *refs: near_kernel(width, total, skip, *refs),
        out_shape=(
            pltpu.VMEM((total + 8, width), jnp.float32),
            jax.ShapeDtypeStruct((8, LANES), jnp.int32),
        ),
        in_specs=[pl.BlockSpec(memory_space=pltpu.SMEM), vmem] + [vmem] * len(parts),
        out_specs=(vmem, vmem),
        scratch_shapes=[
            pltpu.VMEM((8, LANES), jnp.int32),
            pltpu.SMEM((8, LANES), jnp.int32),
            pltpu.SemaphoreType.DMA,
        ],
        compiler_params=pltpu.CompilerParams(vmem_limit_bytes=16 * 2**20),
        name="near",
    )(me, codes, *parts)


def far_kernel(width, total, me, place, low, high, old, image, out, sem):
    base = lax.rem(me[0] + 2, 4) * 2
    put_rows(image, place, low, base, 0, width)
    put_rows(image, place, high, base, low.shape[0], width)
    copy = pltpu.make_async_copy(image.at[pl.ds(0, total)], out, sem)
    copy.start()
    copy.wait()


def far_rows(me, place, parts, image, width, total):
    vmem = pl.BlockSpec(memory_space=pltpu.VMEM)
    smem = pl.BlockSpec(memory_space=pltpu.SMEM)
    return pl.pallas_call(
        lambda *refs: far_kernel(width, total, *refs),
        out_shape=(
            pltpu.VMEM(image.shape, jnp.float32),
            jax.ShapeDtypeStruct((total, width), jnp.float32),
        ),
        in_specs=[smem, smem] + [vmem] * (len(parts) + 1),
        out_specs=(vmem, pl.BlockSpec(memory_space=pl.ANY)),
        scratch_shapes=[pltpu.SemaphoreType.DMA],
        input_output_aliases={2 + len(parts): 0},
        compiler_params=pltpu.CompilerParams(vmem_limit_bytes=16 * 2**20),
        name="far",
    )(me, place, *parts, image)[1]


def local(
    vectors, labels, list_sizes, centroids, split_ids, nearby, owner_map, mover_source, mover_dest
):
    list_dev, rows, width = vectors.shape
    lists_count = lax.axis_size(LISTS)
    help_count = lax.axis_size("help")
    my_line = lax.axis_index(LISTS)
    my_help = lax.axis_index("help")
    first = my_line * list_dev
    start_row = my_help * rows
    splits = split_ids.shape[0]
    local_slots = first + jnp.arange(list_dev, dtype=jnp.int32)
    row_index = start_row + jnp.arange(rows, dtype=jnp.int32)
    valid = row_index[None, :] < list_sizes[:, None]
    moves = mover_source.shape[0]
    ids = jnp.arange(owner_map.shape[0], dtype=jnp.int32)
    devs = jnp.arange(lists_count, dtype=jnp.int32)
    depth = 2

    live = mover_dest >= 0
    slot = jnp.sum(
        jnp.where(mover_dest[:, None] == ids[None, :], owner_map[None, :], 0), axis=1
    )
    dev = jnp.where(live, slot // list_dev, -1)
    order = jnp.arange(moves, dtype=jnp.int32)
    same = (dev[:, None] == dev[None, :]) & (order[:, None] > order[None, :])
    rank = jnp.sum(same.astype(jnp.int32), axis=1)
    to = dev[:, None] == devs[None, :]
    picked = [to & (rank == r)[:, None] for r in range(depth)]
    codes = [
        jnp.sum(jnp.where(p, (slot % list_dev + 1)[:, None], 0), axis=0) for p in picked
    ]
    takes = [jnp.sum(jnp.where(p, mover_source[:, None], 0), axis=0) for p in picked]
    flat_rows = vectors.reshape(list_dev * rows, width)
    sent = [flat_rows[t] for t in takes]

    halves = jnp.stack([(labels == 0) & valid, (labels == 1) & valid], axis=1).astype(jnp.float32)
    partial_value = jnp.einsum("kar,krd->kad", halves, vectors, precision=HIGH)
    counts = jnp.sum(halves, axis=2)
    chunks = lax.axis_size(NEAR)
    cols = width // chunks
    half = list_dev * 2
    lanes = jnp.moveaxis(partial_value.reshape(half, chunks, cols), 1, 0)
    lanes = jnp.concatenate(
        [
            lanes,
            jnp.broadcast_to(counts.reshape(1, half, 1), (chunks, half, 1)),
            jnp.zeros((chunks, half, LANES // half - cols - 1), jnp.float32),
        ],
        axis=2,
    ).reshape(chunks, LANES)
    lanes = jnp.tile(lanes, (lists_count // chunks, 1))
    lane = jnp.arange(LANES, dtype=jnp.int32)
    for r in range(depth):
        lanes = jnp.where(
            lane[None, :] == cols + 1 + r, codes[r].astype(jnp.float32)[:, None], lanes
        )
    bucket = jnp.concatenate([*sent, lanes], axis=1)[:, None, :]
    got = exchanged(bucket, LISTS)

    split_slots = owner_map[split_ids]
    k_ids = jnp.arange(list_dev, dtype=jnp.int32)[:, None]
    key = jnp.where(split_slots[None] % list_dev == k_ids, split_slots[None] // list_dev, -1)
    tail = got[:, :, depth * width :]
    chosen = selected(key.reshape(1, list_dev * splits), tail, cols, depth, help_count)
    over_help = exchanged(chosen, "help")
    sums = jnp.sum(over_help[:, : cols + 1], axis=0)
    means = sums[:cols] / sums[cols:]
    cents = copies(means, NEAR).reshape(width, 2 * splits)

    near_slots = owner_map[nearby]
    hit = jnp.any(near_slots[None, :, :] == local_slots[:, None, None], axis=2)
    penalty = jnp.tile(jnp.where(hit, 0.0, FAR), (1, 2))
    own_cross = jnp.einsum("krd,kd->kr", vectors, centroids, precision=HIGH)
    own_dist = jnp.sum(centroids * centroids, axis=1)[:, None] - 2.0 * own_cross
    gains = scored(vectors, cents, penalty, own_dist, valid.astype(jnp.float32))

    cut = lists_count // 2
    low, high = got[:cut, :, : depth * width], got[cut:, :, : depth * width]
    below_low = turned(low, "help", 1)
    above_high = turned(high, "help", -1)
    below_high = turned(high, "help", 1)
    above_low = turned(low, "help", -1)
    far_low = turned(below_low, "help", 1)
    far_high = turned(above_high, "help", -1)
    arrive_cap = lists_count * help_count * ((depth + list_dev - 1) // list_dev)
    total = list_dev * arrive_cap
    me = my_help[None]
    image, place = near_rows(me, over_help, [low, high, below_low, below_high, above_low, above_high], width, total, cols + 1)
    out = far_rows(me, place, [far_low, far_high], image, width, total)
    return gains, out.reshape(list_dev, arrive_cap, width)


def solution(mesh):
    split = Mesh(
        mesh.devices.reshape(4, 4, 4, 2, mesh.shape["help"]), (*LISTS, "help")
    )
    placed = (
        P(LISTS, "help", None),
        P(LISTS, "help"),
        P(LISTS),
        P(LISTS, None),
        P(),
        P(),
        P(),
        P((*LISTS, "help")),
        P((*LISTS, "help")),
    )

    return jax.shard_map(
        local,
        mesh=split,
        in_specs=placed,
        out_specs=(P(LISTS, "help"), P(LISTS, None, None)),
        check_vma=False,
    )
```

```python
import jax
import jax.numpy as jnp
from jax import lax
from jax.experimental import pallas as pl
from jax.experimental.pallas import tpu as pltpu
from jax.sharding import Mesh
from jax.sharding import PartitionSpec as P

NEAR = ("z_lo", "x", "core")
LISTS = ("z_hi", *NEAR)
LANES = 128
FAR = 1e30
HIGH = lax.Precision.HIGHEST


def exchanged(pieces, axis):
    return lax.all_to_all(pieces, axis, 0, 0, tiled=True)


def copies(shard, axis):
    length = lax.axis_size(axis)
    return exchanged(jnp.broadcast_to(shard[None], (length, *shard.shape)), axis)


def turned(block, axis, step):
    length = lax.axis_size(axis)
    return lax.ppermute(block, axis, [(i, (i + step) % length) for i in range(length)])


def select_kernel(cols, depth, key, tail, out):
    lines = tail.shape[0]
    pairs = key.shape[1]
    rows = tail[:, 0, :].T
    line = lax.broadcasted_iota(jnp.int32, (lines, pairs), 0)
    pick = (line == key[...]).astype(jnp.float32)
    chosen = jnp.dot(rows, pick, precision=HIGH, preferred_element_type=jnp.float32)
    each = LANES // 4
    splits = pairs // 2
    own = [
        chosen[a * each : (a + 1) * each, :splits]
        + chosen[(a + 2) * each : (a + 3) * each, splits:]
        for a in range(2)
    ]
    for y in range(out.shape[0]):
        for a in range(2):
            out[y, :, a * splits : (a + 1) * splits] = own[a]
        for r in range(depth):
            at = cols + 1 + r
            out[y, at : at + 1, :] = rows[at : at + 1, :]


def selected(key, tail, cols, depth, helpers):
    vmem = pl.BlockSpec(memory_space=pltpu.VMEM)
    return pl.pallas_call(
        lambda *refs: select_kernel(cols, depth, *refs),
        out_shape=jax.ShapeDtypeStruct((helpers, LANES // 4, LANES), jnp.float32),
        in_specs=[vmem, vmem],
        out_specs=vmem,
        compiler_params=pltpu.CompilerParams(vmem_limit_bytes=4 * 2**20),
        name="select",
    )(key, tail)


def build_kernel(cols, me, *refs):
    away, (out, *held, spot, scalars, sem, sems) = refs[:6], refs[6:]
    fetches = [
        pltpu.make_async_copy(far, near, sems.at[i])
        for i, (far, near) in enumerate(zip(away, held))
    ]
    for fetch in fetches:
        fetch.start()
    dest, owner, source, sizes, labels, vectors = held
    for fetch in fetches[:3]:
        fetch.wait()
    f32, i32 = jnp.float32, jnp.int32
    lists, rows = labels.shape
    width = vectors.shape[1]
    moves, ids = dest.shape[1], owner.shape[1]

    def spread(shape, dim):
        return lax.broadcasted_iota(i32, shape, dim)

    def eight(row):
        return jnp.broadcast_to(row, (8, row.shape[1])).astype(f32)

    hit = (spread((ids, moves), 0) == dest[...]).astype(f32)
    slot = jnp.dot(eight(owner[...]), hit, precision=HIGH, preferred_element_type=f32)[0:1]
    slot = slot.astype(i32)
    dev = jnp.where(dest[...] >= 0, lax.shift_right_logical(slot, 1), -1)
    code = (jnp.bitwise_and(slot, 1) + 1).astype(f32)
    square = (moves, moves)
    to = (spread(square, 0) == dev).astype(f32)
    sooner = (spread(square, 0) < spread(square, 1)).astype(f32)
    before = jnp.dot(to, sooner, preferred_element_type=f32)
    codes, takes = [], []
    for r in range(2):
        pick = jnp.where(before == float(r), to, 0.0)
        codes.append(jnp.sum(pick * code, axis=1, keepdims=True))
        take = lax.dot_general(
            eight(source[...]), pick, (((1,), (1,)), ((), ())),
            precision=HIGH, preferred_element_type=f32,
        )
        takes.append(take[0:1])
    spot[...] = jnp.concatenate(takes * 4, axis=0).astype(i32)
    copy = pltpu.make_async_copy(spot, scalars, sem)
    copy.start()

    for fetch in fetches[3:]:
        fetch.wait()
    row = spread((1, rows), 1) + me[0] * rows
    kinds = [
        jnp.where(row < sizes[k], labels[k : k + 1, :], 2).astype(f32) for k in range(lists)
    ]
    kinds = jnp.concatenate(kinds * 4, axis=0).T
    chunks = width // cols
    chunk = spread((chunks, width), 1) // cols == spread((chunks, width), 0)
    lane = spread((chunks, LANES), 1)
    pieces, counts = [], jnp.zeros((chunks, LANES), f32)
    each = LANES // 4
    for k in range(lists):
        block = vectors[k * rows : (k + 1) * rows, :]
        for a in range(2):
            mark = kinds[:, k : k + 1] == float(a)
            total = jnp.sum(jnp.where(mark, block, 0.0), axis=0, keepdims=True)
            number = jnp.sum(mark.astype(f32), axis=0, keepdims=True)
            pieces.append(jnp.where(chunk, total, 0.0))
            counts = counts + jnp.where(lane == (2 * k + a) * each + cols, number, 0.0)
    pieces = jnp.concatenate(pieces, axis=0)
    first = pieces.astype(jnp.bfloat16)
    rest = pieces - first.astype(f32)
    second = rest.astype(jnp.bfloat16)
    third = (rest - second.astype(f32)).astype(jnp.bfloat16)
    fold = (spread((width, LANES), 0) % cols == spread((width, LANES), 1)).astype(jnp.bfloat16)
    parts = jnp.concatenate([first, second, third], axis=0)
    folded = jnp.dot(parts, fold, preferred_element_type=f32)
    lines = 4 * chunks
    folded = folded[:lines] + folded[lines : 2 * lines] + folded[2 * lines :]
    tail = counts
    for b in range(4):
        piece = folded[b * chunks : (b + 1) * chunks]
        tail = tail + (pltpu.roll(piece, b * each, 1) if b else piece)
    tail = jnp.concatenate([tail] * (moves // chunks), axis=0)
    lane = spread((moves, LANES), 1)
    for r in range(2):
        tail = jnp.where(lane == cols + 1 + r, codes[r], tail)
    out[:, 0, 2 * width :] = tail

    copy.wait()

    def body(d, carry):
        for r in range(2):
            out[d, :, r * width : (r + 1) * width] = vectors[pl.ds(scalars[r, d], 1), :]
        return carry

    lax.fori_loop(0, moves, body, 0, unroll=4)


def built(me, sizes, source, dest, owner, labels, vectors, cols):
    smem = pl.BlockSpec(memory_space=pltpu.SMEM)
    hbm = pl.BlockSpec(memory_space=pltpu.HBM)
    moves = dest.shape[1]
    away = [dest, owner, source, sizes, labels, vectors]
    held = [(pltpu.SMEM if x is sizes else pltpu.VMEM)(x.shape, x.dtype) for x in away]
    return pl.pallas_call(
        lambda *refs: build_kernel(cols, *refs),
        out_shape=jax.ShapeDtypeStruct((moves, 1, 2 * vectors.shape[1] + LANES), jnp.float32),
        in_specs=[smem] + [hbm] * len(away),
        out_specs=pl.BlockSpec(memory_space=pltpu.VMEM),
        scratch_shapes=held
        + [
            pltpu.VMEM((8, LANES), jnp.int32),
            pltpu.SMEM((8, LANES), jnp.int32),
            pltpu.SemaphoreType.DMA,
            pltpu.SemaphoreType.DMA((len(away),)),
        ],
        compiler_params=pltpu.CompilerParams(vmem_limit_bytes=16 * 2**20),
        name="build",
    )(me, *[pltpu.with_memory_space_constraint(x, pltpu.HBM) for x in away])


def halved(values):
    high = values.astype(jnp.bfloat16)
    return high, (values - high.astype(jnp.float32)).astype(jnp.bfloat16)


def score_kernel(vectors, cents, penalty, own, live, out):
    table = cents[...]
    base = jnp.sum(table * table, axis=0, keepdims=True)
    high, low = halved(table)
    for k in range(vectors.shape[0]):
        rows_high, rows_low = halved(vectors[k])

        def product(left, right):
            return jnp.dot(left, right, preferred_element_type=jnp.float32)

        cross = product(rows_high, low) + product(rows_low, high) + product(rows_high, high)
        dist = base + penalty[k : k + 1, :] - 2.0 * cross
        least = jnp.min(dist.T, axis=0, keepdims=True)
        gain = (own[k : k + 1, :] - least) / vectors.shape[2]
        near = least < 0.5 * FAR
        out[k : k + 1, :] = jnp.where((live[k : k + 1, :] > 0.0) & near, gain, 0.0)


def scored(vectors, cents, penalty, own, live):
    vmem = pl.BlockSpec(memory_space=pltpu.VMEM)
    return pl.pallas_call(
        score_kernel,
        out_shape=jax.ShapeDtypeStruct(own.shape, jnp.float32),
        in_specs=[vmem] * 5,
        out_specs=vmem,
        compiler_params=pltpu.CompilerParams(vmem_limit_bytes=16 * 2**20),
        name="score",
    )(vectors, cents, penalty, own, live)


def put_rows(image, place, ref, base, start, width):
    def body(i, carry):
        for r in range(2):
            p = place[base + r, start + i]
            image[pl.ds(p, 1), :] = ref[i, :, r * width : (r + 1) * width]
        return carry

    lax.fori_loop(0, ref.shape[0], body, 0, unroll=4)


def near_kernel(width, total, skip, me, codes, *refs):
    *parts, image, place, spot, scalars, sem = refs
    lines = codes.shape[2]
    code = jnp.concatenate([codes[y, skip : skip + 2, :] for y in range(4)], axis=0)
    before = (
        lax.broadcasted_iota(jnp.int32, (lines, lines), 0)
        < lax.broadcasted_iota(jnp.int32, (lines, lines), 1)
    ).astype(jnp.float32)
    places = jnp.full(code.shape, float(total), jnp.float32)
    for t in range(2):
        mark = (code == float(t + 1)).astype(jnp.float32)
        per_line = jnp.sum(mark, axis=0, keepdims=True)
        seen = jnp.dot(
            jnp.broadcast_to(per_line, code.shape), before, preferred_element_type=jnp.float32
        )[0:1]
        ahead = []
        for row in range(code.shape[0]):
            ahead.append(seen)
            seen = seen + mark[row : row + 1]
        ahead = jnp.concatenate(ahead, axis=0)
        places = jnp.where(mark > 0.0, ahead + float(t * total // 2), places)
    spot[...] = places.astype(jnp.int32)
    copy = pltpu.make_async_copy(spot, scalars, sem)
    copy.start()
    place[...] = spot[...]
    image[...] = jnp.zeros_like(image)
    copy.wait()
    for at, ref in enumerate(parts):
        base = lax.rem(me[0] + (0, 3, 1)[at // 2], 4) * 2
        put_rows(image, scalars, ref, base, at % 2 * (lines // 2), width)


def near_rows(me, codes, parts, width, total, skip):
    vmem = pl.BlockSpec(memory_space=pltpu.VMEM)
    return pl.pallas_call(
        lambda *refs: near_kernel(width, total, skip, *refs),
        out_shape=(
            pltpu.VMEM((total + 8, width), jnp.float32),
            jax.ShapeDtypeStruct((8, LANES), jnp.int32),
        ),
        in_specs=[pl.BlockSpec(memory_space=pltpu.SMEM), vmem] + [vmem] * len(parts),
        out_specs=(vmem, vmem),
        scratch_shapes=[
            pltpu.VMEM((8, LANES), jnp.int32),
            pltpu.SMEM((8, LANES), jnp.int32),
            pltpu.SemaphoreType.DMA,
        ],
        compiler_params=pltpu.CompilerParams(vmem_limit_bytes=16 * 2**20),
        name="near",
    )(me, codes, *parts)


def far_kernel(width, total, me, place, low, high, old, image, out, sem):
    base = lax.rem(me[0] + 2, 4) * 2
    put_rows(image, place, low, base, 0, width)
    put_rows(image, place, high, base, low.shape[0], width)
    copy = pltpu.make_async_copy(image.at[pl.ds(0, total)], out, sem)
    copy.start()
    copy.wait()


def far_rows(me, place, parts, image, width, total):
    vmem = pl.BlockSpec(memory_space=pltpu.VMEM)
    smem = pl.BlockSpec(memory_space=pltpu.SMEM)
    return pl.pallas_call(
        lambda *refs: far_kernel(width, total, *refs),
        out_shape=(
            pltpu.VMEM(image.shape, jnp.float32),
            jax.ShapeDtypeStruct((total, width), jnp.float32),
        ),
        in_specs=[smem, smem] + [vmem] * (len(parts) + 1),
        out_specs=(vmem, pl.BlockSpec(memory_space=pl.ANY)),
        scratch_shapes=[pltpu.SemaphoreType.DMA],
        input_output_aliases={2 + len(parts): 0},
        compiler_params=pltpu.CompilerParams(vmem_limit_bytes=16 * 2**20),
        name="far",
    )(me, place, *parts, image)[1]


def local(
    vectors, labels, list_sizes, centroids, split_ids, nearby, owner_map, mover_source, mover_dest
):
    list_dev, rows, width = vectors.shape
    lists_count = lax.axis_size(LISTS)
    help_count = lax.axis_size("help")
    my_line = lax.axis_index(LISTS)
    my_help = lax.axis_index("help")
    first = my_line * list_dev
    start_row = my_help * rows
    splits = split_ids.shape[0]
    local_slots = first + jnp.arange(list_dev, dtype=jnp.int32)
    depth = 2

    chunks = lax.axis_size(NEAR)
    cols = width // chunks
    flat_rows = vectors.reshape(list_dev * rows, width)
    me = my_help[None]
    bucket = built(
        me, list_sizes, mover_source[None], mover_dest[None], owner_map[None], labels,
        flat_rows, cols,
    )
    got = exchanged(bucket, LISTS)

    split_slots = owner_map[split_ids]
    k_ids = jnp.arange(list_dev, dtype=jnp.int32)[:, None]
    key = jnp.where(split_slots[None] % list_dev == k_ids, split_slots[None] // list_dev, -1)
    tail = got[:, :, depth * width :]
    chosen = selected(key.reshape(1, list_dev * splits), tail, cols, depth, help_count)
    over_help = exchanged(chosen, "help")
    sums = jnp.sum(over_help[:, : cols + 1], axis=0)
    means = sums[:cols] / sums[cols:]
    cents = copies(means, NEAR).reshape(width, 2 * splits)

    near_slots = owner_map[nearby]
    hit = jnp.any(near_slots[None, :, :] == local_slots[:, None, None], axis=2)
    row_index = start_row + jnp.arange(rows, dtype=jnp.int32)
    live = (row_index[None, :] < list_sizes[:, None]).astype(jnp.float32)
    penalty = jnp.tile(jnp.where(hit, 0.0, FAR), (1, 2))
    own_cross = jnp.einsum("krd,kd->kr", vectors, centroids, precision=HIGH)
    own_dist = jnp.sum(centroids * centroids, axis=1)[:, None] - 2.0 * own_cross
    gains = scored(vectors, cents, penalty, own_dist, live)

    cut = lists_count // 2
    low, high = got[:cut, :, : depth * width], got[cut:, :, : depth * width]
    below_low = turned(low, "help", 1)
    above_high = turned(high, "help", -1)
    below_high = turned(high, "help", 1)
    above_low = turned(low, "help", -1)
    far_low = turned(below_low, "help", 1)
    far_high = turned(above_high, "help", -1)
    arrive_cap = lists_count * help_count * ((depth + list_dev - 1) // list_dev)
    total = list_dev * arrive_cap
    image, place = near_rows(me, over_help, [low, high, below_low, below_high, above_low, above_high], width, total, cols + 1)
    out = far_rows(me, place, [far_low, far_high], image, width, total)
    return gains, out.reshape(list_dev, arrive_cap, width)


def solution(mesh):
    split = Mesh(
        mesh.devices.reshape(4, 4, 4, 2, mesh.shape["help"]), (*LISTS, "help")
    )
    placed = (
        P(LISTS, "help", None),
        P(LISTS, "help"),
        P(LISTS),
        P(LISTS, None),
        P(),
        P(),
        P(),
        P((*LISTS, "help")),
        P((*LISTS, "help")),
    )

    return jax.shard_map(
        local,
        mesh=split,
        in_specs=placed,
        out_specs=(P(LISTS, "help"), P(LISTS, None, None)),
        check_vma=False,
    )
```

```python
import jax
import jax.numpy as jnp
from jax import lax
from jax.experimental import pallas as pl
from jax.experimental.pallas import tpu as pltpu
from jax.sharding import Mesh
from jax.sharding import PartitionSpec as P

PAIR = ("x", "core")
NEAR = ("z_lo", *PAIR)
LISTS = ("z_hi", *NEAR)
LANES = 128
FAR = 1e30
HIGH = lax.Precision.HIGHEST


def exchanged(pieces, axis):
    return lax.all_to_all(pieces, axis, 0, 0, tiled=True)


def copies(shard, axis):
    length = lax.axis_size(axis)
    return exchanged(jnp.broadcast_to(shard[None], (length, *shard.shape)), axis)


def turned(block, axis, step):
    length = lax.axis_size(axis)
    return lax.ppermute(block, axis, [(i, (i + step) % length) for i in range(length)])


def select_kernel(cols, depth, key, tail, out):
    lines = tail.shape[0]
    pairs = key.shape[1]
    rows = tail[:, 0, :].T
    line = lax.broadcasted_iota(jnp.int32, (lines, pairs), 0)
    pick = (line == key[...]).astype(jnp.float32)
    chosen = jnp.dot(rows, pick, precision=HIGH, preferred_element_type=jnp.float32)
    each = LANES // 4
    splits = pairs // 2
    own = [
        chosen[a * each : (a + 1) * each, :splits]
        + chosen[(a + 2) * each : (a + 3) * each, splits:]
        for a in range(2)
    ]
    for y in range(out.shape[0]):
        for a in range(2):
            out[y, :, a * splits : (a + 1) * splits] = own[a]
        for r in range(depth):
            at = cols + 1 + r
            out[y, at : at + 1, :] = rows[at : at + 1, :]


def selected(key, tail, cols, depth, helpers):
    vmem = pl.BlockSpec(memory_space=pltpu.VMEM)
    return pl.pallas_call(
        lambda *refs: select_kernel(cols, depth, *refs),
        out_shape=jax.ShapeDtypeStruct((helpers, LANES // 4, LANES), jnp.float32),
        in_specs=[vmem, vmem],
        out_specs=vmem,
        compiler_params=pltpu.CompilerParams(vmem_limit_bytes=4 * 2**20),
        name="select",
    )(key, tail)


def build_kernel(cols, pairs, me, *refs):
    away, (out, *held, spot, scalars, sem, sems) = refs[:6], refs[6:]
    fetches = [
        pltpu.make_async_copy(far, near, sems.at[i])
        for i, (far, near) in enumerate(zip(away, held))
    ]
    for fetch in fetches:
        fetch.start()
    dest, owner, source, sizes, labels, vectors = held
    for fetch in fetches[:3]:
        fetch.wait()
    f32, i32 = jnp.float32, jnp.int32
    lists, rows = labels.shape
    width = vectors.shape[1]
    moves, ids = dest.shape[1], owner.shape[1]

    def spread(shape, dim):
        return lax.broadcasted_iota(i32, shape, dim)

    def eight(row):
        return jnp.broadcast_to(row, (8, row.shape[1])).astype(f32)

    hit = (spread((ids, moves), 0) == dest[...]).astype(f32)
    slot = jnp.dot(eight(owner[...]), hit, precision=HIGH, preferred_element_type=f32)[0:1]
    slot = slot.astype(i32)
    dev = jnp.where(dest[...] >= 0, lax.shift_right_logical(slot, 1), -1)
    code = (jnp.bitwise_and(slot, 1) + 1).astype(f32)
    square = (moves, moves)
    to = (spread(square, 0) == dev).astype(f32)
    sooner = (spread(square, 0) < spread(square, 1)).astype(f32)
    before = jnp.dot(to, sooner, preferred_element_type=f32)
    codes, takes = [], []
    for r in range(2):
        pick = jnp.where(before == float(r), to, 0.0)
        codes.append(jnp.sum(pick * code, axis=1, keepdims=True))
        take = lax.dot_general(
            eight(source[...]), pick, (((1,), (1,)), ((), ())),
            precision=HIGH, preferred_element_type=f32,
        )
        takes.append(take[0:1])
    spot[...] = jnp.concatenate(takes * 4, axis=0).astype(i32)
    copy = pltpu.make_async_copy(spot, scalars, sem)
    copy.start()

    for fetch in fetches[3:]:
        fetch.wait()
    row = spread((1, rows), 1) + me[0] * rows
    kinds = [
        jnp.where(row < sizes[k], labels[k : k + 1, :], 2).astype(f32) for k in range(lists)
    ]
    kinds = jnp.concatenate(kinds * 4, axis=0).T
    chunks = width // cols
    line = spread((chunks, width), 0)
    line = line % pairs * (chunks // pairs) + line // pairs
    chunk = spread((chunks, width), 1) // cols == line
    lane = spread((chunks, LANES), 1)
    pieces, counts = [], jnp.zeros((chunks, LANES), f32)
    each = LANES // 4
    for k in range(lists):
        block = vectors[k * rows : (k + 1) * rows, :]
        for a in range(2):
            mark = kinds[:, k : k + 1] == float(a)
            total = jnp.sum(jnp.where(mark, block, 0.0), axis=0, keepdims=True)
            number = jnp.sum(mark.astype(f32), axis=0, keepdims=True)
            pieces.append(jnp.where(chunk, total, 0.0))
            counts = counts + jnp.where(lane == (2 * k + a) * each + cols, number, 0.0)
    pieces = jnp.concatenate(pieces, axis=0)
    first = pieces.astype(jnp.bfloat16)
    rest = pieces - first.astype(f32)
    second = rest.astype(jnp.bfloat16)
    third = (rest - second.astype(f32)).astype(jnp.bfloat16)
    fold = (spread((width, LANES), 0) % cols == spread((width, LANES), 1)).astype(jnp.bfloat16)
    parts = jnp.concatenate([first, second, third], axis=0)
    folded = jnp.dot(parts, fold, preferred_element_type=f32)
    lines = 4 * chunks
    folded = folded[:lines] + folded[lines : 2 * lines] + folded[2 * lines :]
    tail = counts
    for b in range(4):
        piece = folded[b * chunks : (b + 1) * chunks]
        tail = tail + (pltpu.roll(piece, b * each, 1) if b else piece)
    tail = jnp.concatenate([tail] * (moves // chunks), axis=0)
    lane = spread((moves, LANES), 1)
    for r in range(2):
        tail = jnp.where(lane == cols + 1 + r, codes[r], tail)
    out[:, 0, 2 * width :] = tail

    copy.wait()

    def body(d, carry):
        for r in range(2):
            out[d, :, r * width : (r + 1) * width] = vectors[pl.ds(scalars[r, d], 1), :]
        return carry

    lax.fori_loop(0, moves, body, 0, unroll=4)


def built(me, sizes, source, dest, owner, labels, vectors, cols, pairs):
    smem = pl.BlockSpec(memory_space=pltpu.SMEM)
    hbm = pl.BlockSpec(memory_space=pltpu.HBM)
    moves = dest.shape[1]
    away = [dest, owner, source, sizes, labels, vectors]
    held = [(pltpu.SMEM if x is sizes else pltpu.VMEM)(x.shape, x.dtype) for x in away]
    return pl.pallas_call(
        lambda *refs: build_kernel(cols, pairs, *refs),
        out_shape=jax.ShapeDtypeStruct((moves, 1, 2 * vectors.shape[1] + LANES), jnp.float32),
        in_specs=[smem] + [hbm] * len(away),
        out_specs=pl.BlockSpec(memory_space=pltpu.VMEM),
        scratch_shapes=held
        + [
            pltpu.VMEM((8, LANES), jnp.int32),
            pltpu.SMEM((8, LANES), jnp.int32),
            pltpu.SemaphoreType.DMA,
            pltpu.SemaphoreType.DMA((len(away),)),
        ],
        compiler_params=pltpu.CompilerParams(vmem_limit_bytes=16 * 2**20),
        name="build",
    )(me, *[pltpu.with_memory_space_constraint(x, pltpu.HBM) for x in away])


def halved(values):
    high = values.astype(jnp.bfloat16)
    return high, (values - high.astype(jnp.float32)).astype(jnp.bfloat16)


def score_kernel(vectors, cents, penalty, own, live, out):
    table = cents[...]
    base = jnp.sum(table * table, axis=0, keepdims=True)
    high, low = halved(table)
    for k in range(vectors.shape[0]):
        rows_high, rows_low = halved(vectors[k])

        def product(left, right):
            return jnp.dot(left, right, preferred_element_type=jnp.float32)

        cross = product(rows_high, low) + product(rows_low, high) + product(rows_high, high)
        dist = base + penalty[k : k + 1, :] - 2.0 * cross
        least = jnp.min(dist.T, axis=0, keepdims=True)
        gain = (own[k : k + 1, :] - least) / vectors.shape[2]
        near = least < 0.5 * FAR
        out[k : k + 1, :] = jnp.where((live[k : k + 1, :] > 0.0) & near, gain, 0.0)


def scored(vectors, cents, penalty, own, live):
    vmem = pl.BlockSpec(memory_space=pltpu.VMEM)
    return pl.pallas_call(
        score_kernel,
        out_shape=jax.ShapeDtypeStruct(own.shape, jnp.float32),
        in_specs=[vmem] * 5,
        out_specs=vmem,
        compiler_params=pltpu.CompilerParams(vmem_limit_bytes=16 * 2**20),
        name="score",
    )(vectors, cents, penalty, own, live)


def put_rows(image, place, ref, base, start, width):
    def body(i, carry):
        for r in range(2):
            p = place[base + r, start + i]
            image[pl.ds(p, 1), :] = ref[i, :, r * width : (r + 1) * width]
        return carry

    lax.fori_loop(0, ref.shape[0], body, 0, unroll=4)


def near_kernel(width, total, skip, me, codes, *refs):
    *parts, image, place, spot, scalars, sem = refs
    lines = codes.shape[2]
    code = jnp.concatenate(
        [codes[me[1] * 4 + y, skip : skip + 2, :] for y in range(4)], axis=0
    )
    before = (
        lax.broadcasted_iota(jnp.int32, (lines, lines), 0)
        < lax.broadcasted_iota(jnp.int32, (lines, lines), 1)
    ).astype(jnp.float32)
    places = jnp.full(code.shape, float(total), jnp.float32)
    for t in range(2):
        mark = (code == float(t + 1)).astype(jnp.float32)
        per_line = jnp.sum(mark, axis=0, keepdims=True)
        seen = jnp.dot(
            jnp.broadcast_to(per_line, code.shape), before, preferred_element_type=jnp.float32
        )[0:1]
        ahead = []
        for row in range(code.shape[0]):
            ahead.append(seen)
            seen = seen + mark[row : row + 1]
        ahead = jnp.concatenate(ahead, axis=0)
        places = jnp.where(mark > 0.0, ahead + float(t * total // 2), places)
    spot[...] = places.astype(jnp.int32)
    copy = pltpu.make_async_copy(spot, scalars, sem)
    copy.start()
    place[...] = spot[...]
    image[...] = jnp.zeros_like(image)
    copy.wait()
    for at, ref in enumerate(parts):
        base = lax.rem(me[0] + (0, 3, 1)[at // 2], 4) * 2
        put_rows(image, scalars, ref, base, at % 2 * (lines // 2), width)


def near_rows(me, codes, parts, width, total, skip):
    vmem = pl.BlockSpec(memory_space=pltpu.VMEM)
    return pl.pallas_call(
        lambda *refs: near_kernel(width, total, skip, *refs),
        out_shape=(
            pltpu.VMEM((total + 8, width), jnp.float32),
            jax.ShapeDtypeStruct((8, LANES), jnp.int32),
        ),
        in_specs=[pl.BlockSpec(memory_space=pltpu.SMEM), vmem] + [vmem] * len(parts),
        out_specs=(vmem, vmem),
        scratch_shapes=[
            pltpu.VMEM((8, LANES), jnp.int32),
            pltpu.SMEM((8, LANES), jnp.int32),
            pltpu.SemaphoreType.DMA,
        ],
        compiler_params=pltpu.CompilerParams(vmem_limit_bytes=16 * 2**20),
        name="near",
    )(me, codes, *parts)


def far_kernel(width, total, me, place, low, high, old, image, out, sem):
    base = lax.rem(me[0] + 2, 4) * 2
    put_rows(image, place, low, base, 0, width)
    put_rows(image, place, high, base, low.shape[0], width)
    copy = pltpu.make_async_copy(image.at[pl.ds(0, total)], out, sem)
    copy.start()
    copy.wait()


def far_rows(me, place, parts, image, width, total):
    vmem = pl.BlockSpec(memory_space=pltpu.VMEM)
    smem = pl.BlockSpec(memory_space=pltpu.SMEM)
    return pl.pallas_call(
        lambda *refs: far_kernel(width, total, *refs),
        out_shape=(
            pltpu.VMEM(image.shape, jnp.float32),
            jax.ShapeDtypeStruct((total, width), jnp.float32),
        ),
        in_specs=[smem, smem] + [vmem] * (len(parts) + 1),
        out_specs=(vmem, pl.BlockSpec(memory_space=pl.ANY)),
        scratch_shapes=[pltpu.SemaphoreType.DMA],
        input_output_aliases={2 + len(parts): 0},
        compiler_params=pltpu.CompilerParams(vmem_limit_bytes=16 * 2**20),
        name="far",
    )(me, place, *parts, image)[1]


def local(
    vectors, labels, list_sizes, centroids, split_ids, nearby, owner_map, mover_source, mover_dest
):
    list_dev, rows, width = vectors.shape
    lists_count = lax.axis_size(LISTS)
    help_count = lax.axis_size("help")
    my_line = lax.axis_index(LISTS)
    my_help = lax.axis_index("help")
    first = my_line * list_dev
    start_row = my_help * rows
    splits = split_ids.shape[0]
    local_slots = first + jnp.arange(list_dev, dtype=jnp.int32)
    depth = 2

    chunks = lax.axis_size(NEAR)
    cols = width // chunks
    flat_rows = vectors.reshape(list_dev * rows, width)
    me = my_help[None]
    bucket = built(
        me, list_sizes, mover_source[None], mover_dest[None], owner_map[None], labels,
        flat_rows, cols, lax.axis_size(PAIR),
    )
    got = exchanged(bucket, LISTS)

    split_slots = owner_map[split_ids]
    k_ids = jnp.arange(list_dev, dtype=jnp.int32)[:, None]
    key = jnp.where(split_slots[None] % list_dev == k_ids, split_slots[None] // list_dev, -1)
    tail = got[:, :, depth * width :]
    groups = lax.axis_size("z_lo")
    chosen = selected(
        key.reshape(1, list_dev * splits), tail, cols, depth, groups * help_count
    )
    over_help = exchanged(chosen, ("z_lo", "help"))
    parts = over_help.reshape(groups, help_count, *over_help.shape[1:])
    sums = jnp.sum(parts[:, :, : cols + 1], axis=1)
    means = sums[:, :cols] / sums[:, cols:]
    means = means.reshape(groups * cols, 2 * splits)
    cents = copies(means, PAIR).reshape(width, 2 * splits)

    near_slots = owner_map[nearby]
    hit = jnp.any(near_slots[None, :, :] == local_slots[:, None, None], axis=2)
    row_index = start_row + jnp.arange(rows, dtype=jnp.int32)
    live = (row_index[None, :] < list_sizes[:, None]).astype(jnp.float32)
    penalty = jnp.tile(jnp.where(hit, 0.0, FAR), (1, 2))
    own_cross = jnp.einsum("krd,kd->kr", vectors, centroids, precision=HIGH)
    own_dist = jnp.sum(centroids * centroids, axis=1)[:, None] - 2.0 * own_cross
    gains = scored(vectors, cents, penalty, own_dist, live)

    cut = lists_count // 2
    low, high = got[:cut, :, : depth * width], got[cut:, :, : depth * width]
    below_low = turned(low, "help", 1)
    above_high = turned(high, "help", -1)
    below_high = turned(high, "help", 1)
    above_low = turned(low, "help", -1)
    far_low = turned(below_low, "help", 1)
    far_high = turned(above_high, "help", -1)
    arrive_cap = lists_count * help_count * ((depth + list_dev - 1) // list_dev)
    total = list_dev * arrive_cap
    where = jnp.stack([my_help, lax.axis_index("z_lo")])
    image, place = near_rows(where, over_help, [low, high, below_low, below_high, above_low, above_high], width, total, cols + 1)
    out = far_rows(me, place, [far_low, far_high], image, width, total)
    return gains, out.reshape(list_dev, arrive_cap, width)


def solution(mesh):
    split = Mesh(
        mesh.devices.reshape(4, 4, 4, 2, mesh.shape["help"]), (*LISTS, "help")
    )
    placed = (
        P(LISTS, "help", None),
        P(LISTS, "help"),
        P(LISTS),
        P(LISTS, None),
        P(),
        P(),
        P(),
        P((*LISTS, "help")),
        P((*LISTS, "help")),
    )

    return jax.shard_map(
        local,
        mesh=split,
        in_specs=placed,
        out_specs=(P(LISTS, "help"), P(LISTS, None, None)),
        check_vma=False,
    )
```

```python
import jax
import jax.numpy as jnp
from jax import lax
from jax.experimental import pallas as pl
from jax.experimental.pallas import tpu as pltpu
from jax.sharding import Mesh
from jax.sharding import PartitionSpec as P

NEAR = ("z_lo", "x", "core")
LISTS = ("z_hi", *NEAR)
LANES = 128
FAR = 1e30
HIGH = lax.Precision.HIGHEST


def exchanged(pieces, axis):
    return lax.all_to_all(pieces, axis, 0, 0, tiled=True)


def copies(shard, axis):
    length = lax.axis_size(axis)
    return exchanged(jnp.broadcast_to(shard[None], (length, *shard.shape)), axis)


def turned(block, axis, step):
    length = lax.axis_size(axis)
    return lax.ppermute(block, axis, [(i, (i + step) % length) for i in range(length)])


def select_kernel(cols, depth, key, tail, out):
    lines = tail.shape[0]
    pairs = key.shape[1]
    rows = tail[:, 0, :].T
    line = lax.broadcasted_iota(jnp.int32, (lines, pairs), 0)
    pick = (line == key[...]).astype(jnp.float32)
    chosen = jnp.dot(rows, pick, precision=HIGH, preferred_element_type=jnp.float32)
    each = LANES // 4
    splits = pairs // 2
    own = [
        chosen[a * each : (a + 1) * each, :splits]
        + chosen[(a + 2) * each : (a + 3) * each, splits:]
        for a in range(2)
    ]
    for y in range(out.shape[0]):
        for a in range(2):
            out[y, :, a * splits : (a + 1) * splits] = own[a]
        for r in range(depth):
            at = cols + 1 + r
            out[y, at : at + 1, :] = rows[at : at + 1, :]


def selected(key, tail, cols, depth, helpers):
    vmem = pl.BlockSpec(memory_space=pltpu.VMEM)
    return pl.pallas_call(
        lambda *refs: select_kernel(cols, depth, *refs),
        out_shape=jax.ShapeDtypeStruct((helpers, LANES // 4, LANES), jnp.float32),
        in_specs=[vmem, vmem],
        out_specs=vmem,
        compiler_params=pltpu.CompilerParams(vmem_limit_bytes=4 * 2**20),
        name="select",
    )(key, tail)


def build_kernel(cols, me, *refs):
    away, (final, *held, out, spot, scalars, sem, sems) = refs[:6], refs[6:]
    fetches = [
        pltpu.make_async_copy(far, near, sems.at[i])
        for i, (far, near) in enumerate(zip(away, held))
    ]
    for fetch in fetches:
        fetch.start()
    dest, owner, source, sizes, labels, vectors = held
    for fetch in fetches[:3]:
        fetch.wait()
    f32, i32 = jnp.float32, jnp.int32
    lists, rows = labels.shape
    width = vectors.shape[1]
    moves, ids = dest.shape[1], owner.shape[1]

    def spread(shape, dim):
        return lax.broadcasted_iota(i32, shape, dim)

    def eight(row):
        return jnp.broadcast_to(row, (8, row.shape[1])).astype(f32)

    hit = (spread((ids, moves), 0) == dest[...]).astype(f32)
    slot = jnp.dot(eight(owner[...]), hit, precision=HIGH, preferred_element_type=f32)[0:1]
    slot = slot.astype(i32)
    dev = jnp.where(dest[...] >= 0, lax.shift_right_logical(slot, 1), -1)
    code = (jnp.bitwise_and(slot, 1) + 1).astype(f32)
    square = (moves, moves)
    to = (spread(square, 0) == dev).astype(f32)
    sooner = (spread(square, 0) < spread(square, 1)).astype(f32)
    before = jnp.dot(to, sooner, preferred_element_type=f32)
    codes, takes = [], []
    for r in range(2):
        pick = jnp.where(before == float(r), to, 0.0)
        codes.append(jnp.sum(pick * code, axis=1, keepdims=True))
        take = lax.dot_general(
            eight(source[...]), pick, (((1,), (1,)), ((), ())),
            precision=HIGH, preferred_element_type=f32,
        )
        takes.append(take[0:1])
    spot[...] = jnp.concatenate(takes * 4, axis=0).astype(i32)
    copy = pltpu.make_async_copy(spot, scalars, sem)
    copy.start()

    for fetch in fetches[3:]:
        fetch.wait()
    row = spread((1, rows), 1) + me[0] * rows
    kinds = [
        jnp.where(row < sizes[k], labels[k : k + 1, :], 2).astype(f32) for k in range(lists)
    ]
    kinds = jnp.concatenate(kinds * 4, axis=0).T
    chunks = width // cols
    chunk = spread((chunks, width), 1) // cols == spread((chunks, width), 0)
    lane = spread((chunks, LANES), 1)
    pieces, counts = [], jnp.zeros((chunks, LANES), f32)
    each = LANES // 4
    for k in range(lists):
        block = vectors[k * rows : (k + 1) * rows, :]
        for a in range(2):
            mark = kinds[:, k : k + 1] == float(a)
            total = jnp.sum(jnp.where(mark, block, 0.0), axis=0, keepdims=True)
            number = jnp.sum(mark.astype(f32), axis=0, keepdims=True)
            pieces.append(jnp.where(chunk, total, 0.0))
            counts = counts + jnp.where(lane == (2 * k + a) * each + cols, number, 0.0)
    pieces = jnp.concatenate(pieces, axis=0)
    first = pieces.astype(jnp.bfloat16)
    rest = pieces - first.astype(f32)
    second = rest.astype(jnp.bfloat16)
    third = (rest - second.astype(f32)).astype(jnp.bfloat16)
    fold = (spread((width, LANES), 0) % cols == spread((width, LANES), 1)).astype(jnp.bfloat16)
    parts = jnp.concatenate([first, second, third], axis=0)
    folded = jnp.dot(parts, fold, preferred_element_type=f32)
    lines = 4 * chunks
    folded = folded[:lines] + folded[lines : 2 * lines] + folded[2 * lines :]
    tail = counts
    for b in range(4):
        piece = folded[b * chunks : (b + 1) * chunks]
        tail = tail + (pltpu.roll(piece, b * each, 1) if b else piece)
    tail = jnp.concatenate([tail] * (moves // chunks), axis=0)
    lane = spread((moves, LANES), 1)
    for r in range(2):
        tail = jnp.where(lane == cols + 1 + r, codes[r], tail)
    out[:, 0, 2 * width :] = tail

    copy.wait()

    def body(d, carry):
        for r in range(2):
            out[d, :, r * width : (r + 1) * width] = vectors[pl.ds(scalars[r, d], 1), :]
        return carry

    stores = []
    for part in range(4):
        lines = moves // 4
        lax.fori_loop(part * lines, (part + 1) * lines, body, 0, unroll=8)
        block = pl.ds(part * lines, lines)
        stores.append(
            pltpu.make_async_copy(out.at[block], final.at[block], sems.at[len(away) + part])
        )
        stores[-1].start()
    for store in stores:
        store.wait()


def built(me, sizes, source, dest, owner, labels, vectors, cols):
    smem = pl.BlockSpec(memory_space=pltpu.SMEM)
    hbm = pl.BlockSpec(memory_space=pltpu.HBM)
    shape = (dest.shape[1], 1, 2 * vectors.shape[1] + LANES)
    away = [dest, owner, source, sizes, labels, vectors]
    held = [(pltpu.SMEM if x is sizes else pltpu.VMEM)(x.shape, x.dtype) for x in away]
    return pl.pallas_call(
        lambda *refs: build_kernel(cols, *refs),
        out_shape=jax.ShapeDtypeStruct(shape, jnp.float32),
        in_specs=[smem] + [hbm] * len(away),
        out_specs=hbm,
        scratch_shapes=held
        + [
            pltpu.VMEM(shape, jnp.float32),
            pltpu.VMEM((8, LANES), jnp.int32),
            pltpu.SMEM((8, LANES), jnp.int32),
            pltpu.SemaphoreType.DMA,
            pltpu.SemaphoreType.DMA((len(away) + 4,)),
        ],
        compiler_params=pltpu.CompilerParams(vmem_limit_bytes=16 * 2**20),
        name="build",
    )(me, *[pltpu.with_memory_space_constraint(x, pltpu.HBM) for x in away])


def halved(values):
    high = values.astype(jnp.bfloat16)
    return high, (values - high.astype(jnp.float32)).astype(jnp.bfloat16)


def score_kernel(vectors, cents, penalty, own, live, out):
    table = cents[...]
    base = jnp.sum(table * table, axis=0, keepdims=True)
    high, low = halved(table)
    for k in range(vectors.shape[0]):
        rows_high, rows_low = halved(vectors[k])

        def product(left, right):
            return jnp.dot(left, right, preferred_element_type=jnp.float32)

        cross = product(rows_high, low) + product(rows_low, high) + product(rows_high, high)
        dist = base + penalty[k : k + 1, :] - 2.0 * cross
        least = jnp.min(dist.T, axis=0, keepdims=True)
        gain = (own[k : k + 1, :] - least) / vectors.shape[2]
        near = least < 0.5 * FAR
        out[k : k + 1, :] = jnp.where((live[k : k + 1, :] > 0.0) & near, gain, 0.0)


def scored(vectors, cents, penalty, own, live):
    vmem = pl.BlockSpec(memory_space=pltpu.VMEM)
    return pl.pallas_call(
        score_kernel,
        out_shape=jax.ShapeDtypeStruct(own.shape, jnp.float32),
        in_specs=[vmem] * 5,
        out_specs=vmem,
        compiler_params=pltpu.CompilerParams(vmem_limit_bytes=16 * 2**20),
        name="score",
    )(vectors, cents, penalty, own, live)


def put_rows(image, place, ref, base, start, width):
    def body(i, carry):
        for r in range(2):
            p = place[base + r, start + i]
            image[pl.ds(p, 1), :] = ref[i, :, r * width : (r + 1) * width]
        return carry

    lax.fori_loop(0, ref.shape[0], body, 0, unroll=8)


def near_kernel(width, total, skip, me, codes, *refs):
    *parts, image, place, spot, scalars, sem = refs
    lines = codes.shape[2]
    code = jnp.concatenate([codes[y, skip : skip + 2, :] for y in range(4)], axis=0)
    before = (
        lax.broadcasted_iota(jnp.int32, (lines, lines), 0)
        < lax.broadcasted_iota(jnp.int32, (lines, lines), 1)
    ).astype(jnp.float32)
    places = jnp.full(code.shape, float(total), jnp.float32)
    for t in range(2):
        mark = (code == float(t + 1)).astype(jnp.float32)
        per_line = jnp.sum(mark, axis=0, keepdims=True)
        seen = jnp.dot(
            jnp.broadcast_to(per_line, code.shape), before, preferred_element_type=jnp.float32
        )[0:1]
        ahead = []
        for row in range(code.shape[0]):
            ahead.append(seen)
            seen = seen + mark[row : row + 1]
        ahead = jnp.concatenate(ahead, axis=0)
        places = jnp.where(mark > 0.0, ahead + float(t * total // 2), places)
    spot[...] = places.astype(jnp.int32)
    copy = pltpu.make_async_copy(spot, scalars, sem)
    copy.start()
    place[...] = spot[...]
    image[...] = jnp.zeros_like(image)
    copy.wait()
    for at, ref in enumerate(parts):
        base = lax.rem(me[0] + (0, 3, 1)[at // 2], 4) * 2
        put_rows(image, scalars, ref, base, at % 2 * (lines // 2), width)


def near_rows(me, codes, parts, width, total, skip):
    vmem = pl.BlockSpec(memory_space=pltpu.VMEM)
    return pl.pallas_call(
        lambda *refs: near_kernel(width, total, skip, *refs),
        out_shape=(
            pltpu.VMEM((total + 8, width), jnp.float32),
            jax.ShapeDtypeStruct((8, LANES), jnp.int32),
        ),
        in_specs=[pl.BlockSpec(memory_space=pltpu.SMEM), vmem] + [vmem] * len(parts),
        out_specs=(vmem, vmem),
        scratch_shapes=[
            pltpu.VMEM((8, LANES), jnp.int32),
            pltpu.SMEM((8, LANES), jnp.int32),
            pltpu.SemaphoreType.DMA,
        ],
        compiler_params=pltpu.CompilerParams(vmem_limit_bytes=16 * 2**20),
        name="near",
    )(me, codes, *[pltpu.with_memory_space_constraint(x, pltpu.VMEM) for x in parts])


def far_kernel(width, total, me, place, low, high, old, image, out, sem):
    base = lax.rem(me[0] + 2, 4) * 2
    put_rows(image, place, low, base, 0, width)
    put_rows(image, place, high, base, low.shape[0], width)
    copy = pltpu.make_async_copy(image.at[pl.ds(0, total)], out, sem)
    copy.start()
    copy.wait()


def far_rows(me, place, parts, image, width, total):
    vmem = pl.BlockSpec(memory_space=pltpu.VMEM)
    smem = pl.BlockSpec(memory_space=pltpu.SMEM)
    return pl.pallas_call(
        lambda *refs: far_kernel(width, total, *refs),
        out_shape=(
            pltpu.VMEM(image.shape, jnp.float32),
            jax.ShapeDtypeStruct((total, width), jnp.float32),
        ),
        in_specs=[smem, smem] + [vmem] * (len(parts) + 1),
        out_specs=(vmem, pl.BlockSpec(memory_space=pl.ANY)),
        scratch_shapes=[pltpu.SemaphoreType.DMA],
        input_output_aliases={2 + len(parts): 0},
        compiler_params=pltpu.CompilerParams(vmem_limit_bytes=16 * 2**20),
        name="far",
    )(me, place, *[pltpu.with_memory_space_constraint(x, pltpu.VMEM) for x in parts], image)[1]


def local(
    vectors, labels, list_sizes, centroids, split_ids, nearby, owner_map, mover_source, mover_dest
):
    list_dev, rows, width = vectors.shape
    lists_count = lax.axis_size(LISTS)
    help_count = lax.axis_size("help")
    my_line = lax.axis_index(LISTS)
    my_help = lax.axis_index("help")
    first = my_line * list_dev
    start_row = my_help * rows
    splits = split_ids.shape[0]
    local_slots = first + jnp.arange(list_dev, dtype=jnp.int32)
    depth = 2

    chunks = lax.axis_size(NEAR)
    cols = width // chunks
    flat_rows = vectors.reshape(list_dev * rows, width)
    me = my_help[None]
    bucket = built(
        me, list_sizes, mover_source[None], mover_dest[None], owner_map[None], labels,
        flat_rows, cols,
    )
    got = exchanged(bucket, LISTS)

    split_slots = owner_map[split_ids]
    k_ids = jnp.arange(list_dev, dtype=jnp.int32)[:, None]
    key = jnp.where(split_slots[None] % list_dev == k_ids, split_slots[None] // list_dev, -1)
    tail = got[:, :, depth * width :]
    chosen = selected(key.reshape(1, list_dev * splits), tail, cols, depth, help_count)
    over_help = exchanged(chosen, "help")
    sums = jnp.sum(over_help[:, : cols + 1], axis=0)
    means = sums[:cols] / sums[cols:]
    cents = copies(means, NEAR).reshape(width, 2 * splits)

    near_slots = owner_map[nearby]
    hit = jnp.any(near_slots[None, :, :] == local_slots[:, None, None], axis=2)
    row_index = start_row + jnp.arange(rows, dtype=jnp.int32)
    live = (row_index[None, :] < list_sizes[:, None]).astype(jnp.float32)
    penalty = jnp.tile(jnp.where(hit, 0.0, FAR), (1, 2))
    own_cross = jnp.einsum("krd,kd->kr", vectors, centroids, precision=HIGH)
    own_dist = jnp.sum(centroids * centroids, axis=1)[:, None] - 2.0 * own_cross
    gains = scored(vectors, cents, penalty, own_dist, live)

    cut = lists_count // 2
    low, high = got[:cut, :, : depth * width], got[cut:, :, : depth * width]
    below_low = turned(low, "help", 1)
    above_high = turned(high, "help", -1)
    below_high = turned(high, "help", 1)
    above_low = turned(low, "help", -1)
    far_low = turned(below_low, "help", 1)
    far_high = turned(above_high, "help", -1)
    arrive_cap = lists_count * help_count * ((depth + list_dev - 1) // list_dev)
    total = list_dev * arrive_cap
    image, place = near_rows(me, over_help, [low, high, below_low, below_high, above_low, above_high], width, total, cols + 1)
    out = far_rows(me, place, [far_low, far_high], image, width, total)
    return gains, out.reshape(list_dev, arrive_cap, width)


def solution(mesh):
    split = Mesh(
        mesh.devices.reshape(4, 4, 4, 2, mesh.shape["help"]), (*LISTS, "help")
    )
    placed = (
        P(LISTS, "help", None),
        P(LISTS, "help"),
        P(LISTS),
        P(LISTS, None),
        P(),
        P(),
        P(),
        P((*LISTS, "help")),
        P((*LISTS, "help")),
    )

    return jax.shard_map(
        local,
        mesh=split,
        in_specs=placed,
        out_specs=(P(LISTS, "help"), P(LISTS, None, None)),
        check_vma=False,
    )
```

```python
import jax
import jax.numpy as jnp
from jax import lax
from jax.experimental import pallas as pl
from jax.experimental.pallas import tpu as pltpu
from jax.sharding import Mesh
from jax.sharding import PartitionSpec as P

PAIR = ("x", "core")
NEAR = ("z_lo", *PAIR)
LISTS = ("z_hi", *NEAR)
LANES = 128
FAR = 1e30
HIGH = lax.Precision.HIGHEST


def exchanged(pieces, axis):
    return lax.all_to_all(pieces, axis, 0, 0, tiled=True)


def copies(shard, axis):
    length = lax.axis_size(axis)
    return exchanged(jnp.broadcast_to(shard[None], (length, *shard.shape)), axis)


def turned(block, axis, step):
    length = lax.axis_size(axis)
    return lax.ppermute(block, axis, [(i, (i + step) % length) for i in range(length)])


def select_kernel(cols, depth, key, tail, out):
    lines = tail.shape[0]
    pairs = key.shape[1]
    rows = tail[:, 0, :].T
    line = lax.broadcasted_iota(jnp.int32, (lines, pairs), 0)
    pick = (line == key[...]).astype(jnp.float32)
    chosen = jnp.dot(rows, pick, precision=HIGH, preferred_element_type=jnp.float32)
    each = LANES // 4
    splits = pairs // 2
    own = [
        chosen[a * each : (a + 1) * each, :splits]
        + chosen[(a + 2) * each : (a + 3) * each, splits:]
        for a in range(2)
    ]
    for y in range(out.shape[0]):
        for a in range(2):
            out[y, :, a * splits : (a + 1) * splits] = own[a]
        for r in range(depth):
            at = cols + 1 + r
            out[y, at : at + 1, :] = rows[at : at + 1, :]


def selected(key, tail, cols, depth, helpers):
    vmem = pl.BlockSpec(memory_space=pltpu.VMEM)
    return pl.pallas_call(
        lambda *refs: select_kernel(cols, depth, *refs),
        out_shape=jax.ShapeDtypeStruct((helpers, LANES // 4, LANES), jnp.float32),
        in_specs=[vmem, vmem],
        out_specs=vmem,
        compiler_params=pltpu.CompilerParams(vmem_limit_bytes=4 * 2**20),
        name="select",
    )(key, tail)


def build_kernel(cols, pairs, me, *refs):
    away, (final, *held, out, spot, scalars, sem, sems) = refs[:6], refs[6:]
    fetches = [
        pltpu.make_async_copy(far, near, sems.at[i])
        for i, (far, near) in enumerate(zip(away, held))
    ]
    for fetch in fetches:
        fetch.start()
    dest, owner, source, sizes, labels, vectors = held
    for fetch in fetches[:3]:
        fetch.wait()
    f32, i32 = jnp.float32, jnp.int32
    lists, rows = labels.shape
    width = vectors.shape[1]
    moves, ids = dest.shape[1], owner.shape[1]

    def spread(shape, dim):
        return lax.broadcasted_iota(i32, shape, dim)

    def eight(row):
        return jnp.broadcast_to(row, (8, row.shape[1])).astype(f32)

    hit = (spread((ids, moves), 0) == dest[...]).astype(f32)
    slot = jnp.dot(eight(owner[...]), hit, precision=HIGH, preferred_element_type=f32)[0:1]
    slot = slot.astype(i32)
    dev = jnp.where(dest[...] >= 0, lax.shift_right_logical(slot, 1), -1)
    code = (jnp.bitwise_and(slot, 1) + 1).astype(f32)
    square = (moves, moves)
    to = (spread(square, 0) == dev).astype(f32)
    sooner = (spread(square, 0) < spread(square, 1)).astype(f32)
    before = jnp.dot(to, sooner, preferred_element_type=f32)
    codes, takes = [], []
    for r in range(2):
        pick = jnp.where(before == float(r), to, 0.0)
        codes.append(jnp.sum(pick * code, axis=1, keepdims=True))
        take = lax.dot_general(
            eight(source[...]), pick, (((1,), (1,)), ((), ())),
            precision=HIGH, preferred_element_type=f32,
        )
        takes.append(take[0:1])
    spot[...] = jnp.concatenate(takes * 4, axis=0).astype(i32)
    copy = pltpu.make_async_copy(spot, scalars, sem)
    copy.start()

    for fetch in fetches[3:]:
        fetch.wait()
    row = spread((1, rows), 1) + me[0] * rows
    kinds = [
        jnp.where(row < sizes[k], labels[k : k + 1, :], 2).astype(f32) for k in range(lists)
    ]
    kinds = jnp.concatenate(kinds * 4, axis=0).T
    chunks = width // cols
    line = spread((chunks, width), 0)
    line = line % pairs * (chunks // pairs) + line // pairs
    chunk = spread((chunks, width), 1) // cols == line
    lane = spread((chunks, LANES), 1)
    pieces, counts = [], jnp.zeros((chunks, LANES), f32)
    each = LANES // 4
    for k in range(lists):
        block = vectors[k * rows : (k + 1) * rows, :]
        for a in range(2):
            mark = kinds[:, k : k + 1] == float(a)
            total = jnp.sum(jnp.where(mark, block, 0.0), axis=0, keepdims=True)
            number = jnp.sum(mark.astype(f32), axis=0, keepdims=True)
            pieces.append(jnp.where(chunk, total, 0.0))
            counts = counts + jnp.where(lane == (2 * k + a) * each + cols, number, 0.0)
    pieces = jnp.concatenate(pieces, axis=0)
    first = pieces.astype(jnp.bfloat16)
    rest = pieces - first.astype(f32)
    second = rest.astype(jnp.bfloat16)
    third = (rest - second.astype(f32)).astype(jnp.bfloat16)
    fold = (spread((width, LANES), 0) % cols == spread((width, LANES), 1)).astype(jnp.bfloat16)
    parts = jnp.concatenate([first, second, third], axis=0)
    folded = jnp.dot(parts, fold, preferred_element_type=f32)
    lines = 4 * chunks
    folded = folded[:lines] + folded[lines : 2 * lines] + folded[2 * lines :]
    tail = counts
    for b in range(4):
        piece = folded[b * chunks : (b + 1) * chunks]
        tail = tail + (pltpu.roll(piece, b * each, 1) if b else piece)
    tail = jnp.concatenate([tail] * (moves // chunks), axis=0)
    lane = spread((moves, LANES), 1)
    for r in range(2):
        tail = jnp.where(lane == cols + 1 + r, codes[r], tail)
    out[:, 0, 2 * width :] = tail

    copy.wait()

    def body(d, carry):
        for r in range(2):
            out[d, :, r * width : (r + 1) * width] = vectors[pl.ds(scalars[r, d], 1), :]
        return carry

    stores = []
    for part in range(4):
        lines = moves // 4
        lax.fori_loop(part * lines, (part + 1) * lines, body, 0, unroll=8)
        block = pl.ds(part * lines, lines)
        stores.append(
            pltpu.make_async_copy(out.at[block], final.at[block], sems.at[len(away) + part])
        )
        stores[-1].start()
    for store in stores:
        store.wait()


def built(me, sizes, source, dest, owner, labels, vectors, cols, pairs):
    smem = pl.BlockSpec(memory_space=pltpu.SMEM)
    hbm = pl.BlockSpec(memory_space=pltpu.HBM)
    shape = (dest.shape[1], 1, 2 * vectors.shape[1] + LANES)
    away = [dest, owner, source, sizes, labels, vectors]
    held = [(pltpu.SMEM if x is sizes else pltpu.VMEM)(x.shape, x.dtype) for x in away]
    return pl.pallas_call(
        lambda *refs: build_kernel(cols, pairs, *refs),
        out_shape=jax.ShapeDtypeStruct(shape, jnp.float32),
        in_specs=[smem] + [hbm] * len(away),
        out_specs=hbm,
        scratch_shapes=held
        + [
            pltpu.VMEM(shape, jnp.float32),
            pltpu.VMEM((8, LANES), jnp.int32),
            pltpu.SMEM((8, LANES), jnp.int32),
            pltpu.SemaphoreType.DMA,
            pltpu.SemaphoreType.DMA((len(away) + 4,)),
        ],
        compiler_params=pltpu.CompilerParams(vmem_limit_bytes=16 * 2**20),
        name="build",
    )(me, *[pltpu.with_memory_space_constraint(x, pltpu.HBM) for x in away])


def halved(values):
    high = values.astype(jnp.bfloat16)
    return high, (values - high.astype(jnp.float32)).astype(jnp.bfloat16)


def score_kernel(vectors, cents, penalty, own, live, out):
    table = cents[...]
    base = jnp.sum(table * table, axis=0, keepdims=True)
    high, low = halved(table)
    for k in range(vectors.shape[0]):
        rows_high, rows_low = halved(vectors[k])

        def product(left, right):
            return jnp.dot(left, right, preferred_element_type=jnp.float32)

        cross = product(rows_high, low) + product(rows_low, high) + product(rows_high, high)
        dist = base + penalty[k : k + 1, :] - 2.0 * cross
        least = jnp.min(dist.T, axis=0, keepdims=True)
        gain = (own[k : k + 1, :] - least) / vectors.shape[2]
        near = least < 0.5 * FAR
        out[k : k + 1, :] = jnp.where((live[k : k + 1, :] > 0.0) & near, gain, 0.0)


def scored(vectors, cents, penalty, own, live):
    vmem = pl.BlockSpec(memory_space=pltpu.VMEM)
    return pl.pallas_call(
        score_kernel,
        out_shape=jax.ShapeDtypeStruct(own.shape, jnp.float32),
        in_specs=[vmem] * 5,
        out_specs=vmem,
        compiler_params=pltpu.CompilerParams(vmem_limit_bytes=16 * 2**20),
        name="score",
    )(vectors, cents, penalty, own, live)


def put_rows(image, place, ref, base, start, width):
    def body(i, carry):
        for r in range(2):
            p = place[base + r, start + i]
            image[pl.ds(p, 1), :] = ref[i, :, r * width : (r + 1) * width]
        return carry

    lax.fori_loop(0, ref.shape[0], body, 0, unroll=8)


def near_kernel(width, total, skip, me, codes, *refs):
    *parts, image, place, spot, scalars, sem = refs
    lines = codes.shape[2]
    code = jnp.concatenate(
        [codes[me[1] * 4 + y, skip : skip + 2, :] for y in range(4)], axis=0
    )
    before = (
        lax.broadcasted_iota(jnp.int32, (lines, lines), 0)
        < lax.broadcasted_iota(jnp.int32, (lines, lines), 1)
    ).astype(jnp.float32)
    places = jnp.full(code.shape, float(total), jnp.float32)
    for t in range(2):
        mark = (code == float(t + 1)).astype(jnp.float32)
        per_line = jnp.sum(mark, axis=0, keepdims=True)
        seen = jnp.dot(
            jnp.broadcast_to(per_line, code.shape), before, preferred_element_type=jnp.float32
        )[0:1]
        ahead = []
        for row in range(code.shape[0]):
            ahead.append(seen)
            seen = seen + mark[row : row + 1]
        ahead = jnp.concatenate(ahead, axis=0)
        places = jnp.where(mark > 0.0, ahead + float(t * total // 2), places)
    spot[...] = places.astype(jnp.int32)
    copy = pltpu.make_async_copy(spot, scalars, sem)
    copy.start()
    place[...] = spot[...]
    image[...] = jnp.zeros_like(image)
    copy.wait()
    for at, ref in enumerate(parts):
        base = lax.rem(me[0] + (0, 3, 1)[at // 2], 4) * 2
        put_rows(image, scalars, ref, base, at % 2 * parts[0].shape[0], width)


def near_rows(me, codes, parts, width, total, skip):
    vmem = pl.BlockSpec(memory_space=pltpu.VMEM)
    return pl.pallas_call(
        lambda *refs: near_kernel(width, total, skip, *refs),
        out_shape=(
            pltpu.VMEM((total + 8, width), jnp.float32),
            jax.ShapeDtypeStruct((8, LANES), jnp.int32),
        ),
        in_specs=[pl.BlockSpec(memory_space=pltpu.SMEM), vmem] + [vmem] * len(parts),
        out_specs=(vmem, vmem),
        scratch_shapes=[
            pltpu.VMEM((8, LANES), jnp.int32),
            pltpu.SMEM((8, LANES), jnp.int32),
            pltpu.SemaphoreType.DMA,
        ],
        compiler_params=pltpu.CompilerParams(vmem_limit_bytes=16 * 2**20),
        name="near",
    )(me, codes, *parts)


def far_kernel(width, total, me, place, low, high, old, image, out, sem):
    base = lax.rem(me[0] + 2, 4) * 2
    put_rows(image, place, low, base, 0, width)
    put_rows(image, place, high, base, low.shape[0], width)
    copy = pltpu.make_async_copy(image.at[pl.ds(0, total)], out, sem)
    copy.start()
    copy.wait()


def far_rows(me, place, parts, image, width, total):
    vmem = pl.BlockSpec(memory_space=pltpu.VMEM)
    smem = pl.BlockSpec(memory_space=pltpu.SMEM)
    return pl.pallas_call(
        lambda *refs: far_kernel(width, total, *refs),
        out_shape=(
            pltpu.VMEM(image.shape, jnp.float32),
            jax.ShapeDtypeStruct((total, width), jnp.float32),
        ),
        in_specs=[smem, smem] + [vmem] * (len(parts) + 1),
        out_specs=(vmem, pl.BlockSpec(memory_space=pl.ANY)),
        scratch_shapes=[pltpu.SemaphoreType.DMA],
        input_output_aliases={2 + len(parts): 0},
        compiler_params=pltpu.CompilerParams(vmem_limit_bytes=16 * 2**20),
        name="far",
    )(me, place, *parts, image)[1]


def local(
    vectors, labels, list_sizes, centroids, split_ids, nearby, owner_map, mover_source, mover_dest
):
    list_dev, rows, width = vectors.shape
    lists_count = lax.axis_size(LISTS)
    help_count = lax.axis_size("help")
    my_line = lax.axis_index(LISTS)
    my_help = lax.axis_index("help")
    first = my_line * list_dev
    start_row = my_help * rows
    splits = split_ids.shape[0]
    local_slots = first + jnp.arange(list_dev, dtype=jnp.int32)
    depth = 2

    chunks = lax.axis_size(NEAR)
    cols = width // chunks
    flat_rows = vectors.reshape(list_dev * rows, width)
    me = my_help[None]
    bucket = built(
        me, list_sizes, mover_source[None], mover_dest[None], owner_map[None], labels,
        flat_rows, cols, lax.axis_size(PAIR),
    )
    got = exchanged(bucket, LISTS)

    split_slots = owner_map[split_ids]
    k_ids = jnp.arange(list_dev, dtype=jnp.int32)[:, None]
    key = jnp.where(split_slots[None] % list_dev == k_ids, split_slots[None] // list_dev, -1)
    tail = got[:, :, depth * width :]
    groups = lax.axis_size("z_lo")
    chosen = selected(
        key.reshape(1, list_dev * splits), tail, cols, depth, groups * help_count
    )
    over_help = exchanged(chosen, ("z_lo", "help"))
    parts = over_help.reshape(groups, help_count, *over_help.shape[1:])
    sums = jnp.sum(parts[:, :, : cols + 1], axis=1)
    means = sums[:, :cols] / sums[:, cols:]
    means = means.reshape(groups * cols, 2 * splits)
    cents = copies(means, PAIR).reshape(width, 2 * splits)

    near_slots = owner_map[nearby]
    hit = jnp.any(near_slots[None, :, :] == local_slots[:, None, None], axis=2)
    row_index = start_row + jnp.arange(rows, dtype=jnp.int32)
    live = (row_index[None, :] < list_sizes[:, None]).astype(jnp.float32)
    penalty = jnp.tile(jnp.where(hit, 0.0, FAR), (1, 2))
    own_cross = jnp.einsum("krd,kd->kr", vectors, centroids, precision=HIGH)
    own_dist = jnp.sum(centroids * centroids, axis=1)[:, None] - 2.0 * own_cross
    gains = scored(vectors, cents, penalty, own_dist, live)

    cut = lists_count * 9 // 16
    low, high = got[:cut, :, : depth * width], got[cut:, :, : depth * width]
    below_low = turned(low, "help", 1)
    above_high = turned(high, "help", -1)
    below_high = turned(high, "help", 1)
    above_low = turned(low, "help", -1)
    far_low = turned(below_low, "help", 1)
    far_high = turned(above_high, "help", -1)
    arrive_cap = lists_count * help_count * ((depth + list_dev - 1) // list_dev)
    total = list_dev * arrive_cap
    where = jnp.stack([my_help, lax.axis_index("z_lo")])
    image, place = near_rows(where, over_help, [low, high, below_low, below_high, above_low, above_high], width, total, cols + 1)
    out = far_rows(me, place, [far_low, far_high], image, width, total)
    return gains, out.reshape(list_dev, arrive_cap, width)


def solution(mesh):
    split = Mesh(
        mesh.devices.reshape(4, 4, 4, 2, mesh.shape["help"]), (*LISTS, "help")
    )
    placed = (
        P(LISTS, "help", None),
        P(LISTS, "help"),
        P(LISTS),
        P(LISTS, None),
        P(),
        P(),
        P(),
        P((*LISTS, "help")),
        P((*LISTS, "help")),
    )

    return jax.shard_map(
        local,
        mesh=split,
        in_specs=placed,
        out_specs=(P(LISTS, "help"), P(LISTS, None, None)),
        check_vma=False,
    )
```
